256 devices in a mesh: dir: 32 (over z, y_hi, core), freq: 8 (over x, y_lo).
Axes of the slice: x: 4, y: 4 (y_hi: 2, y_lo: 2; y = y_hi * 2 + y_lo), z: 8, core: 2. Of those that a mesh axis runs over, the one named last changes fastest.
Arguments:
- spectrum: float32 [64, 48, 8192], P('dir', 'freq'), may hold values from 0.1 to 1
- neighbours: int32 [6, 8192], replicated, may hold values from 0 to 8191
- edge_angle: float32 [6, 8192], replicated, may hold values from -3.140625 to 3.140625
- edge_coef: float32 [6, 8192], replicated, may hold values from 0.02 to 0.1
- land_mask: int32 [8192], replicated, may hold values 0 or 1
- dia_offsets: int32 [2, 3], replicated, may hold values from 1 to 6, as said below
- dia_coef: float32 [3], replicated, may hold values from 0.2 to 1
- space_order: int32 [8192], replicated, may hold values from 0 to 8191, each once
- wind_speed: float32 [8192], P(('dir', 'freq')), may hold values from 0.5 to 2.5
- wind_dir: float32 [8192], P(('dir', 'freq')), may hold values from -3.140625 to 3.140625
Outputs:
- new_spectrum: float32 [64, 48, 8192], P(None, None, ('dir', 'freq'))
The draws below stay inside these ranges and needn't reach their ends.
Inputs may be any that keep to these rules, and one draw needn't show every extreme that they name: `dia_offsets`: row 0 holds direction offsets from 1 to 6, one of them 6; row 1 holds frequency offsets from 1 to 2, one of them 2.
All inputs are finite; a program needn't handle non-finite values.
Results may differ from the reference program's by a relative error of at most 0.00061.
Values may be sent and summed in bfloat16 or wider, within the bound.
No kernel may reach another device: no remote copies, remote signals or barrier semaphores. Data moves between devices by JAX's collectives and lax.ppermute only.
A program may use at most 64 MiB of HBM per device.

```python
import math
import jax
import jax.numpy as jnp
from jax import lax

NDIR = 64
NFREQ = 48
NPTS = 8192
NEIGH = 6
NQ = 3
DSPAN = 6
FSPAN = 2


def draw_dia_offsets(key, part):
    first, second, third, fourth = jax.random.split(jax.random.fold_in(key, 17), 4)
    dirs = jax.random.randint(first, (NQ,), 1, DSPAN + 1)
    freqs = jax.random.randint(second, (NQ,), 1, FSPAN + 1)
    slot_dir = jax.random.randint(third, (), 0, NQ)
    slot_freq = jax.random.randint(fourth, (), 0, NQ)
    rows = jnp.arange(NQ)
    dirs = jnp.where(rows == slot_dir, DSPAN, dirs)
    freqs = jnp.where(rows == slot_freq, FSPAN, freqs)
    return jnp.stack([dirs, freqs]).astype(jnp.int32)


def place_ends(drawn, stream_key, smallest, largest):
    index_at = [jax.random.randint(jax.random.fold_in(stream_key, axis), (), 0, length) for axis, length in enumerate(drawn.shape)]
    longest = drawn.shape.index(max(drawn.shape))
    neighbour = index_at[:longest] + [(index_at[longest] + 1) % drawn.shape[longest]] + index_at[longest + 1:]
    return drawn.at[tuple(index_at)].set(smallest).at[tuple(neighbour)].set(largest)


def steps_of(own_key, dims, shards, low, top_value):
    factor_of, own = 1.0, jax.random.fold_in(own_key, 6)
    for position, parts in shards:
        draws = jnp.exp(jax.random.uniform(jax.random.fold_in(own, position), (parts,), jnp.float32, low / len(shards), top_value / len(shards)))
        factor_of = factor_of * jnp.repeat(draws, dims[position] // parts).reshape([-1 if axis == position else 1 for axis in range(len(dims))])
    return factor_of


def setup_inputs(seed: int = 0) -> dict:
    splits = jax.random.split(jax.random.key(seed), 11)
    spectrum = jnp.clip(jnp.exp(math.log(1.0) - 2.3025851 * jax.random.uniform(splits[0], (NDIR, NFREQ, NPTS), jnp.float32) ** steps_of(splits[0], (NDIR, NFREQ, NPTS), ((0, 32), (1, 8)), -0.2, 0.2)), 0.1, 1.0)
    neighbours = place_ends(jax.random.randint(splits[1], (NEIGH, NPTS), 0, NPTS), jax.random.fold_in(splits[1], 1), 0, NPTS - 1).astype(jnp.int32)
    edge_angle = jnp.clip(jax.random.uniform(splits[2], (NEIGH, NPTS), jnp.float32, -3.140625, 3.140625), -3.140625, 3.140625)
    edge_coef = jnp.clip(jnp.exp(jax.random.uniform(splits[3], (NEIGH, NPTS), jnp.float32, math.log(0.02), math.log(0.1))), 0.02, 0.1)
    land_mask = place_ends((jax.random.randint(splits[4], (NPTS,), 0, 5) < 4).astype(jnp.int32), jax.random.fold_in(splits[4], 1), 0, 1)
    dia_offsets = draw_dia_offsets(jax.random.fold_in(splits[10], 71), 0)
    dia_coef = jnp.clip(jnp.exp(jax.random.uniform(splits[6], (NQ,), jnp.float32, math.log(0.2), math.log(1.0))), 0.2, 1.0)
    space_order = jax.random.permutation(splits[7], NPTS).astype(jnp.int32)
    wind_speed = jnp.clip(jnp.exp(math.log(2.5) - 1.609438 * jax.random.uniform(splits[8], (NPTS,), jnp.float32) ** steps_of(splits[8], (NPTS,), ((0, 256),), -0.2, 0.2)), 0.5, 2.5)
    wind_dir = jnp.clip(jax.random.uniform(splits[9], (NPTS,), jnp.float32, -3.140625, 3.140625), -3.140625, 3.140625)
    return dict(spectrum=spectrum, neighbours=neighbours, edge_angle=edge_angle, edge_coef=edge_coef, land_mask=land_mask, dia_offsets=dia_offsets, dia_coef=dia_coef, space_order=space_order, wind_speed=wind_speed, wind_dir=wind_dir)


SIG_LO = 0.35
SIG_HI = 2.8
DT_NL = 0.1
CDS = 0.05
APM = 0.4
BETA = 0.05
INV_FLOOR = 0.01


def frequencies(first, count, total):
    index = (first + jnp.arange(count, dtype=jnp.int32)).astype(jnp.float32)
    return SIG_LO * jnp.exp(index * (math.log(SIG_HI / SIG_LO) / (total - 1)))


def propagate(field, neighbours, edge_angle, edge_coef, wetness, theta, speed):
    masked = field * wetness[None, None, :]
    total = field
    for k in range(neighbours.shape[0]):
        beside = jnp.take(masked, neighbours[k], axis=2)
        geometry = edge_coef[k][None, :] * jnp.maximum(jnp.cos(theta[:, None] - edge_angle[k][None, :]), 0.0)
        total = total + speed[None, :, None] * geometry[:, None, :] * (beside - field)
    return total


def nonlinear(window, center, dpad, offsets, dia_coef):
    ndirs, nfreqs, npoints = center.shape
    total = jnp.zeros(center.shape, jnp.float32)
    for q in range(dia_coef.shape[0]):
        dshift = offsets[0, q].astype(jnp.int32)
        fshift = offsets[1, q].astype(jnp.int32)
        zero_start = jnp.zeros((), jnp.int32)
        upper = lax.dynamic_slice(window, ((dpad + dshift).astype(jnp.int32), (FSPAN + fshift).astype(jnp.int32), zero_start), (ndirs, nfreqs, npoints)).astype(jnp.float32)
        lower = lax.dynamic_slice(window, ((dpad - dshift).astype(jnp.int32), (FSPAN - fshift).astype(jnp.int32), zero_start), (ndirs, nfreqs, npoints)).astype(jnp.float32)
        delta = center * center * (upper + lower) - 2.0 * center * upper * lower
        total = total + dia_coef[q] * delta
    return total


def point_rates(field, sigma):
    weight = 1.0 / (field.shape[0] * field.shape[1])
    etot = jnp.sum(field, axis=(0, 1)) * weight
    inverse = jnp.sum(field / sigma[None, :, None], axis=(0, 1)) * weight
    msig = jnp.clip(etot / jnp.maximum(inverse, INV_FLOOR), SIG_LO, SIG_HI)
    steep = etot * msig ** 4 / APM
    return msig, steep


def apply_sources(field, sigma, theta, msig, steep, wind_speed, wind_dir):
    rate = CDS * (sigma[None, :, None] / msig[None, None, :]) ** 2 * msig[None, None, :] * steep[None, None, :] ** 2
    alignment = jnp.cos(theta[:, None] - wind_dir[None, :])
    growth = BETA * sigma[None, :, None] * jnp.maximum(wind_speed[None, None, :] * sigma[None, :, None] * alignment[:, None, :] - 1.0, 0.0)
    return field * (1.0 + growth) / (1.0 + rate)


def reference(spectrum, neighbours, edge_angle, edge_coef, land_mask, dia_offsets, dia_coef, space_order, wind_speed, wind_dir):
    ndirs = spectrum.shape[0]
    wetness = land_mask.astype(jnp.float32)
    sigma = frequencies(0, NFREQ, NFREQ)
    speed = 0.5 / sigma
    old = spectrum.astype(jnp.bfloat16)
    padded = jnp.concatenate([old[ndirs - DSPAN:], old, old[:DSPAN]], axis=0)
    padded = jnp.pad(padded, ((0, 0), (FSPAN, FSPAN), (0, 0)))

    def one_direction(index):
        theta = (2.0 * math.pi / ndirs) * index.astype(jnp.float32)[None]
        field = lax.dynamic_slice_in_dim(spectrum, index, 1, 0)
        moved = propagate(field, neighbours, edge_angle, edge_coef, wetness, theta, speed)
        window = lax.dynamic_slice_in_dim(padded, index, 2 * DSPAN + 1, 0)
        center = lax.dynamic_slice_in_dim(old, index, 1, 0).astype(jnp.float32)
        transfer = nonlinear(window, center, DSPAN, dia_offsets, dia_coef)
        updated = wetness[None, None, :] * (moved + DT_NL * transfer)
        return jnp.take(updated[0], space_order, axis=1)

    relaid = lax.map(one_direction, jnp.arange(ndirs, dtype=jnp.int32))
    msig, steep = point_rates(relaid, sigma)

    def finish(index):
        theta = (2.0 * math.pi / ndirs) * index.astype(jnp.float32)[None]
        field = lax.dynamic_slice_in_dim(relaid, index, 1, 0)
        return apply_sources(field, sigma, theta, msig, steep, wind_speed, wind_dir)[0]

    return lax.map(finish, jnp.arange(ndirs, dtype=jnp.int32))
```

```python
import functools
import math

import jax
import jax.numpy as jnp
from jax import lax
from jax.experimental import pallas as pl
from jax.experimental.pallas import tpu as pltpu
from jax.sharding import PartitionSpec as P

NFREQ = 48
DSPAN = 6
FSPAN = 2

SIG_LO = 0.35
SIG_HI = 2.8
DT_NL = 0.1
CDS = 0.05
APM = 0.4
BETA = 0.05
INV_FLOOR = 0.01

LANES = 128
TILE = 256
CENTRE = 0.5


def sigma_of(index):
    return SIG_LO * jnp.exp(index.astype(jnp.float32) * (math.log(SIG_HI / SIG_LO) / (NFREQ - 1)))


def one_hot(low, ramp):
    return jnp.where(ramp == low.astype(jnp.float32).astype(jnp.bfloat16), 1.0, 0.0).astype(jnp.bfloat16)


def local_kernel(
    ndirs, spec_at, nbr_at, angle_at, coef_at, mask_at, order_at, out,
    spec, nbr, angle, coef, mask, order, arrived, field, pickf, pick, geom, wet, keepf, keep, ramp
):
    dirs, freqs, npoints = 2, spec.shape[0], spec.shape[2]
    pairs = [(spec_at, spec), (mask_at, mask), (angle_at, angle)]
    pairs += [(coef_at, coef), (nbr_at, nbr), (order_at, order)]
    copies = [
        pltpu.make_async_copy(src, dst, arrived.at[n]) for n, (src, dst) in enumerate(pairs)
    ]
    for copy in copies:
        copy.start()
    tiles = npoints // TILE
    first_dir = lax.axis_index("dir") * dirs
    first_freq = lax.axis_index("freq") * freqs
    sub = lax.broadcasted_iota(jnp.int32, (8, TILE), 0)
    lane = lax.broadcasted_iota(jnp.int32, (8, LANES), 1)
    speed = 0.5 / sigma_of(first_freq + sub)
    ramp[...] = lax.broadcasted_iota(jnp.int32, (TILE, TILE), 0).astype(jnp.float32).astype(jnp.bfloat16)
    pad = jnp.zeros((8 - freqs, TILE), jnp.float32)

    for copy in copies[:4]:
        copy.wait()

    def stage(t, carry):
        at = pl.ds(pl.multiple_of(t * TILE, TILE), TILE)
        wet_row = mask[:, at].astype(jnp.float32)
        wet[:, at] = wet_row
        for i in range(dirs):
            rows = [spec[f, pl.ds(i, 1), at] for f in range(freqs)]
            value = jnp.concatenate(rows + [pad], axis=0)
            field[i, :, at] = value
            shown = value * wet_row - CENTRE
            spot = pl.ds(i * freqs * tiles + t, freqs, stride=tiles)
            for c in range(TILE // LANES):
                pickf[c, spot, :] = shown[:freqs, c * LANES : (c + 1) * LANES]
            theta = (2.0 * math.pi / ndirs) * (first_dir + i).astype(jnp.float32)
            bearing = jnp.cos(theta - angle[:, at])
            geom[i, :, at] = coef[:, at] * jnp.maximum(bearing, 0.0)
        return carry

    lax.fori_loop(0, tiles, stage, 0)
    for c in range(TILE // LANES):
        pick[:, c * LANES : (c + 1) * LANES] = pickf[c].astype(jnp.bfloat16)

    groups = tiles // 8

    copies[4].wait()

    def advect(t, carry):
        at = pl.ds(pl.multiple_of(t * TILE, TILE), TILE)
        total = [jnp.zeros((8, TILE), jnp.float32) for _ in range(dirs * freqs)]
        weight = [jnp.zeros((1, TILE), jnp.float32) for _ in range(dirs)]
        for k in range(nbr.shape[0]):
            index = nbr[k : k + 1, at]
            low = jnp.bitwise_and(index, TILE - 1)
            high = jnp.broadcast_to(jnp.right_shift(index, 8), (8, TILE))
            found = jnp.dot(pick[...], one_hot(low, ramp[...]), preferred_element_type=jnp.float32)
            match = [high == sub + 8 * h for h in range(groups)]
            for i in range(dirs):
                row = geom[i, k : k + 1, at]
                weight[i] = weight[i] + row
                for f in range(freqs):
                    r = i * freqs + f
                    chosen = jnp.zeros((8, TILE), jnp.float32)
                    for h in range(groups):
                        start = r * tiles + 8 * h
                        chosen = jnp.where(match[h], found[start : start + 8], chosen)
                    total[r] = total[r] + row * chosen
        wet_row = wet[:, at]
        kept, rest = [], []
        for i in range(dirs):
            value = field[i, :, at]
            rows = [
                jnp.sum(total[i * freqs + f], axis=0, keepdims=True) for f in range(freqs)
            ]
            inflow = jnp.concatenate(rows + [pad], axis=0)
            moved = value + speed * (inflow + weight[i] * (CENTRE - value))
            old = value.astype(jnp.bfloat16).astype(jnp.float32)
            kept.append(wet_row * old)
            rest.append(wet_row * (moved - old))
        for g, part in enumerate(kept + rest):
            keepf[pl.ds(pl.multiple_of(t * 32, 32) + 8 * g, 8), :] = part
        return carry

    lax.fori_loop(0, tiles, advect, 0, unroll=4)
    keep[...] = keepf[...].astype(jnp.bfloat16)

    copies[5].wait()

    def swap(t, carry):
        at = pl.ds(pl.multiple_of(t * TILE, TILE), TILE)
        index = order[:, at]
        low = jnp.bitwise_and(index, TILE - 1)
        high = jnp.broadcast_to(jnp.right_shift(index, 8), (8, TILE))
        found = jnp.dot(keep[...], one_hot(low, ramp[...]), preferred_element_type=jnp.float32)
        part = [jnp.zeros((8, TILE), jnp.float32) for _ in range(4)]
        for h in range(tiles):
            match = high == h
            for g in range(4):
                start = 32 * h + 8 * g
                part[g] = jnp.where(match, found[start : start + 8], part[g])
        for c in range(TILE // LANES):
            v = [x[:, c * LANES : (c + 1) * LANES] for x in part]
            left = lane < 64
            w0 = jnp.where(left, v[0], pltpu.roll(v[2], 64, 1))
            w2 = jnp.where(left, pltpu.roll(v[0], 64, 1), v[2])
            w1 = jnp.where(left, v[1], pltpu.roll(v[3], 64, 1))
            w3 = jnp.where(left, pltpu.roll(v[1], 64, 1), v[3])
            even = jnp.bitwise_and(lane, 32) == 0
            blocks = [
                jnp.where(even, w0, pltpu.roll(w1, 32, 1)),
                jnp.where(even, pltpu.roll(w0, 96, 1), w1),
                jnp.where(even, w2, pltpu.roll(w3, 32, 1)),
                jnp.where(even, pltpu.roll(w2, 96, 1), w3),
            ]
            for b in range(4):
                out[t * 8 + c * 4 + b] = blocks[b].astype(jnp.bfloat16)
        return carry

    lax.fori_loop(0, tiles, swap, 0, unroll=4)


def finish_kernel(
    freq_blocks, offsets, strength, wind_speed, wind_dir, blocks, out, table, relaid, rows
):
    nblocks, _, _ = blocks.shape
    pairs = nblocks // freq_blocks
    reach = DSPAN // 2
    freqs = NFREQ // freq_blocks
    low_pad = 8
    lane = lax.broadcasted_iota(jnp.int32, (NFREQ, LANES), 1)
    first = lane < 32
    half = lane < 64
    ndirs = 2 * pairs
    npts = 32

    edge = jnp.zeros((8, LANES), jnp.float32)
    for parity in range(2):
        for s in range(pairs + 2 * reach):
            table[parity, s, 0:8] = edge
            table[parity, s, low_pad + NFREQ : low_pad + NFREQ + 8] = edge

    def unpack(s, carry):
        for b in range(freq_blocks):
            piece = blocks[s * freq_blocks + b].astype(jnp.float32)
            table[0, s + reach, low_pad + b * freqs : low_pad + (b + 1) * freqs] = piece[:freqs]
        body = table[0, s + reach, low_pad : low_pad + NFREQ]
        turned = jnp.where(first, pltpu.roll(body, LANES - 32, 1), pltpu.roll(body, 32, 1))
        table[1, s + reach, low_pad : low_pad + NFREQ] = turned
        return carry

    lax.fori_loop(0, pairs, unpack, 0)
    for parity in range(2):
        for s in range(reach):
            table[parity, s] = table[parity, s + pairs]
            table[parity, s + pairs + reach] = table[parity, s + reach]

    def transfer(s, carry):
        total = carry
        body = table[0, s + reach, low_pad : low_pad + NFREQ]
        moved = body + pltpu.roll(body, 64, 1)
        change = jnp.zeros((NFREQ, LANES), jnp.float32)
        for q in range(strength.shape[0]):
            d = offsets[0, q]
            m = offsets[1, q]
            odd = jnp.bitwise_and(d, 1)

            def shifted(by, start):
                near = s + reach + jnp.right_shift(by, 1)
                far = s + reach + jnp.right_shift(by + 1, 1)
                at = pl.ds(low_pad + start, NFREQ)
                return jnp.where(first, table[odd, near, at], table[odd, far, at])

            upper = shifted(d, m)
            lower = shifted(-d, -m)
            delta = body * body * (upper + lower) - 2.0 * body * upper * lower
            change = change + strength[q] * delta
        value = moved + DT_NL * change
        relaid[s] = value
        return total + value

    total = lax.fori_loop(0, pairs, transfer, jnp.zeros((NFREQ, LANES), jnp.float32))

    sigma = sigma_of(lax.broadcasted_iota(jnp.int32, (NFREQ, LANES), 0))
    weight = 1.0 / (ndirs * NFREQ)

    def over_dirs(x):
        x = jnp.sum(x, axis=0, keepdims=True)
        x = jnp.broadcast_to(x, (8, LANES))
        lane8 = lane[:8]
        x = x + jnp.where(lane8 < 32, pltpu.roll(x, LANES - 32, 1), pltpu.roll(x, 32, 1))
        return x[:1]

    etot = over_dirs(total) * weight
    inverse = over_dirs(total / sigma) * weight
    msig = jnp.clip(etot / jnp.maximum(inverse, INV_FLOOR), SIG_LO, SIG_HI)
    steep = etot * (msig * msig * msig * msig) / APM
    ratio = sigma / msig
    rate = CDS * (ratio * ratio) * msig * (steep * steep)
    damp = 1.0 / (1.0 + rate)
    wind = jnp.concatenate([wind_speed[...]] * 4, axis=1) * sigma
    towards = jnp.concatenate([wind_dir[...]] * 4, axis=1)
    step = lax.broadcasted_iota(jnp.int32, (pairs, LANES), 0) * 2 + jnp.bitwise_and(
        jnp.right_shift(lax.broadcasted_iota(jnp.int32, (pairs, LANES), 1), 5), 1
    )
    rows[...] = jnp.cos((2.0 * math.pi / ndirs) * step.astype(jnp.float32) - towards)
    push = BETA * sigma

    def grow(s, carry):
        growth = push * jnp.maximum(wind * rows[pl.ds(s, 1), :] - 1.0, 0.0)
        value = relaid[s] * (1.0 + growth) * damp
        out[s] = value[:, :64]
        return carry

    lax.fori_loop(0, pairs, grow, 0)


def local_call(
    ndirs, parts, spectrum, neighbours, edge_angle, edge_coef, land_mask, space_order
):
    dirs, freqs, npoints = spectrum.shape
    tiles = npoints // TILE
    near = neighbours.shape[0]
    vmem = pl.BlockSpec(memory_space=pltpu.VMEM)
    return pl.pallas_call(
        functools.partial(local_kernel, ndirs),
        out_shape=jax.ShapeDtypeStruct((parts, 8, LANES), jnp.bfloat16),
        in_specs=[pl.BlockSpec(memory_space=pltpu.MemorySpace.HBM)] * 6,
        out_specs=vmem,
        scratch_shapes=[
            pltpu.VMEM((freqs, dirs, npoints), jnp.float32),
            pltpu.VMEM((near, npoints), jnp.int32),
            pltpu.VMEM((near, npoints), jnp.float32),
            pltpu.VMEM((near, npoints), jnp.float32),
            pltpu.VMEM((1, npoints), jnp.int32),
            pltpu.VMEM((1, npoints), jnp.int32),
            pltpu.SemaphoreType.DMA((6,)),
            pltpu.VMEM((dirs, 8, npoints), jnp.float32),
            pltpu.VMEM((TILE // LANES, dirs * freqs * tiles, LANES), jnp.float32),
            pltpu.VMEM((dirs * freqs * tiles, TILE), jnp.bfloat16),
            pltpu.VMEM((dirs, near, npoints), jnp.float32),
            pltpu.VMEM((1, npoints), jnp.float32),
            pltpu.VMEM((32 * tiles, TILE), jnp.float32),
            pltpu.VMEM((32 * tiles, TILE), jnp.bfloat16),
            pltpu.VMEM((TILE, TILE), jnp.bfloat16),
        ],
        compiler_params=pltpu.CompilerParams(vmem_limit_bytes=40 * 1024 * 1024),
        name="local_step",
    )(
        *(
            pltpu.with_memory_space_constraint(x, pltpu.MemorySpace.HBM)
            for x in (
                spectrum.transpose(1, 0, 2),
                neighbours,
                edge_angle,
                edge_coef,
                land_mask.reshape(1, npoints),
                space_order.reshape(1, npoints),
            )
        )
    )


def on_device(
    spectrum,
    neighbours,
    edge_angle,
    edge_coef,
    land_mask,
    dia_offsets,
    dia_coef,
    space_order,
    wind_speed,
    wind_dir,
):
    dirs, freqs, npoints = spectrum.shape
    nd, nf = lax.axis_size("dir"), lax.axis_size("freq")
    parts = nd * nf
    vmem = pl.BlockSpec(memory_space=pltpu.VMEM)
    smem = pl.BlockSpec(memory_space=pltpu.SMEM)
    blocks = local_call(
        nd * dirs, parts, spectrum, neighbours, edge_angle, edge_coef, land_mask, space_order
    )
    blocks = lax.all_to_all(blocks, ("dir", "freq"), split_axis=0, concat_axis=0, tiled=True)
    npts = npoints // parts
    done = pl.pallas_call(
        functools.partial(finish_kernel, nf),
        out_shape=jax.ShapeDtypeStruct((nd, NFREQ, 2 * npts), jnp.float32),
        in_specs=[smem, smem, vmem, vmem, vmem],
        out_specs=vmem,
        scratch_shapes=[
            pltpu.VMEM((2, nd + DSPAN, NFREQ + 16, LANES), jnp.float32),
            pltpu.VMEM((nd, NFREQ, LANES), jnp.float32),
            pltpu.VMEM((nd, LANES), jnp.float32),
        ],
        compiler_params=pltpu.CompilerParams(vmem_limit_bytes=40 * 1024 * 1024),
        name="finish_step",
    )(dia_offsets, dia_coef, wind_speed.reshape(1, npts), wind_dir.reshape(1, npts), blocks)
    done = done.reshape(nd, NFREQ, 2, npts).transpose(0, 2, 1, 3)
    return done.reshape(2 * nd, NFREQ, npts)


def solution(mesh):
    in_specs = (
        P("dir", "freq", None),
        P(),
        P(),
        P(),
        P(),
        P(),
        P(),
        P(),
        P(("dir", "freq")),
        P(("dir", "freq")),
    )
    out_specs = P(None, None, ("dir", "freq"))
    return jax.shard_map(
        on_device, mesh=mesh, in_specs=in_specs, out_specs=out_specs, check_vma=False
    )
```

```python
import functools
import math

import jax
import jax.numpy as jnp
from jax import lax
from jax.experimental import pallas as pl
from jax.experimental.pallas import tpu as pltpu
from jax.sharding import PartitionSpec as P

NFREQ = 48
DSPAN = 6
FSPAN = 2

SIG_LO = 0.35
SIG_HI = 2.8
DT_NL = 0.1
CDS = 0.05
APM = 0.4
BETA = 0.05
INV_FLOOR = 0.01

LANES = 128
TILE = 256
STAGE, ADVECT, SWAP = 2, 4, 8
CENTRE = 0.5


def sigma_of(index):
    return SIG_LO * jnp.exp(index.astype(jnp.float32) * (math.log(SIG_HI / SIG_LO) / (NFREQ - 1)))


def one_hot(low, ramp):
    one, none = jnp.ones((), jnp.bfloat16), jnp.zeros((), jnp.bfloat16)
    return jnp.where(ramp == low.astype(jnp.float32).astype(jnp.bfloat16), one, none)


def local_kernel(
    ndirs, spec_at, nbr_at, angle_at, coef_at, mask_at, order_at, out,
    spec, nbr, angle, coef, mask, order, arrived, field, pickf, pick, keepf, keep, ramp, *sums
):
    freqs, dirs, npoints = spec.shape
    tiles = npoints // TILE
    near = nbr.shape[0]
    first_dir = lax.axis_index("dir") * dirs
    first_freq = lax.axis_index("freq") * freqs
    pairs = [(spec_at, spec), (mask_at, mask), (nbr_at, nbr)]
    pairs += [(angle_at, angle), (coef_at, coef), (order_at, order)]
    copies = [
        pltpu.make_async_copy(src, dst, arrived.at[n]) for n, (src, dst) in enumerate(pairs)
    ]
    for copy in copies:
        copy.start()
    sub = lax.broadcasted_iota(jnp.int32, (8, TILE), 0)
    lane = lax.broadcasted_iota(jnp.int32, (8, LANES), 1)
    speed = 0.5 / sigma_of(first_freq + sub)
    ramp[...] = lax.broadcasted_iota(jnp.int32, (TILE, TILE), 0).astype(jnp.float32).astype(jnp.bfloat16)
    pad = jnp.zeros((8 - freqs, TILE), jnp.float32)
    for copy in copies[:2]:
        copy.wait()

    def span(t):
        return pl.ds(pl.multiple_of(t * TILE, TILE), TILE)

    def stage(t, carry):
        at = span(t)
        wet_row = mask[:, at].astype(jnp.float32)
        for i in range(dirs):
            rows = [spec[f, pl.ds(i, 1), at] for f in range(freqs)]
            value = jnp.concatenate(rows + [pad], axis=0)
            field[i, :, at] = value
            shown = value * wet_row - CENTRE
            spot = pl.ds(i * freqs * tiles + t, freqs, stride=tiles)
            for c in range(TILE // LANES):
                pickf[c, spot, :] = shown[:freqs, c * LANES : (c + 1) * LANES]
        return carry

    lax.fori_loop(0, tiles, stage, 0, unroll=STAGE)
    for c in range(TILE // LANES):
        pick[:, c * LANES : (c + 1) * LANES] = pickf[c].astype(jnp.bfloat16)
    for copy in copies[2:5]:
        copy.wait()

    def split(index):
        low = jnp.bitwise_and(index, TILE - 1)
        high = jnp.broadcast_to(jnp.right_shift(index, 8), (8, TILE))
        return one_hot(low, ramp[...]), high

    def issue(job, table, accs, index, chunk):
        unit, slot = job % 2, job // 2 % 2
        hot, high = split(index)
        pltpu.matmul_push_rhs(hot, slot, unit)
        for c, acc in enumerate(accs[unit][slot]):
            rows = table[c * chunk : (c + 1) * chunk, :]
            pltpu.matmul_acc_lhs(acc, rows, load_staged_rhs=slot if c == 0 else None)
        return high

    groups = tiles // 8
    chunk = 3 * tiles
    count = dirs * freqs // 3
    accs = [[sums[(u * 2 + v) * count : (u * 2 + v + 1) * count] for v in range(2)] for u in range(2)]

    def advect(step, carry):
        jobs = [(u, k) for u in range(ADVECT) for k in range(near)]
        highs = {}

        def start(n):
            u, k = jobs[n]
            highs[n] = issue(n, pick, accs, nbr[k : k + 1, span(step * ADVECT + u)], chunk)

        start(0)
        start(1)
        for n, (u, k) in enumerate(jobs):
            t = step * ADVECT + u
            at = span(t)
            if k == 0:
                total = [jnp.zeros((8, TILE), jnp.float32) for _ in range(dirs * freqs)]
                geom = []
                for i in range(dirs):
                    theta = (2.0 * math.pi / ndirs) * (first_dir + i).astype(jnp.float32)
                    bearing = jnp.cos(theta - angle[:, at])
                    geom.append(coef[:, at] * jnp.maximum(bearing, 0.0))
            high = highs.pop(n)
            match = [high == sub + 8 * h for h in range(groups)]
            rows = [geom[i][k : k + 1] for i in range(dirs)]
            unit, slot = n % 2, n // 2 % 2
            for c, acc in enumerate(accs[unit][slot]):
                found = pltpu.matmul_pop(acc)
                for x in range(3):
                    r = c * 3 + x
                    chosen = jnp.zeros((8, TILE), jnp.float32)
                    for h in range(groups):
                        begin = x * tiles + 8 * h
                        chosen = jnp.where(match[h], found[begin : begin + 8], chosen)
                    total[r] = total[r] + rows[r // freqs] * chosen
            if n + 2 < len(jobs):
                start(n + 2)
            if k == near - 1:
                wet_row = mask[:, at].astype(jnp.float32)
                kept, rest = [], []
                for i in range(dirs):
                    value = field[i, :, at]
                    weight = jnp.sum(geom[i], axis=0, keepdims=True)
                    lines = [
                        jnp.sum(total[i * freqs + f], axis=0, keepdims=True) for f in range(freqs)
                    ]
                    inflow = jnp.concatenate(lines + [pad], axis=0)
                    moved = value + speed * (inflow + weight * (CENTRE - value))
                    old = value.astype(jnp.bfloat16).astype(jnp.float32)
                    kept.append((wet_row * old)[:freqs])
                    rest.append((wet_row * (moved - old))[:freqs])
                width = 2 * dirs * freqs
                spot = pl.ds(pl.multiple_of(t * width, 8), width)
                keepf[spot, :] = jnp.concatenate(kept + rest, axis=0)
        return carry

    lax.fori_loop(0, tiles // ADVECT, advect, 0)
    keep[...] = keepf[...].astype(jnp.bfloat16)
    copies[5].wait()
    width = 2 * dirs * freqs

    def swap(step, carry):
        jobs = list(range(SWAP))
        highs = {}
        hots = {}
        accs = [[*sums[: 2 * count]], [*sums[2 * count :]]]

        def push(n):
            hots[n], highs[n] = split(order[:, span(step * SWAP + n)])
            pltpu.matmul_push_rhs(hots[n], n // 2 % 2, n % 2)

        def multiply(n, c):
            rows = keep[c * chunk : (c + 1) * chunk, :]
            slot = n // 2 % 2 if c == 0 else None
            pltpu.matmul_acc_lhs(accs[n % 2][c], rows, load_staged_rhs=slot)

        for n in jobs[:2]:
            push(n)
            for c in range(2 * count):
                multiply(n, c)
        for n in jobs:
            high = highs.pop(n)
            part = [jnp.zeros((8, TILE), jnp.float32) for _ in range(width // 8)]
            if n + 2 < len(jobs):
                push(n + 2)
            for c in range(2 * count):
                found = pltpu.matmul_pop(accs[n % 2][c])
                if n + 2 < len(jobs):
                    multiply(n + 2, c)
                for x in range(chunk // width):
                    match = high == c * (chunk // width) + x
                    for g in range(width // 8):
                        begin = x * width + 8 * g
                        part[g] = jnp.where(match, found[begin : begin + 8], part[g])
            whole = jnp.concatenate(part, axis=0)
            whole = [whole[g * freqs : (g + 1) * freqs] for g in range(2 * dirs)]
            whole = [jnp.concatenate([x, pad], axis=0) for x in whole]
            for c in range(TILE // LANES):
                v = [x[:, c * LANES : (c + 1) * LANES] for x in whole]
                left = lane < 64
                w0 = jnp.where(left, v[0], pltpu.roll(v[2], 64, 1))
                w2 = jnp.where(left, pltpu.roll(v[0], 64, 1), v[2])
                w1 = jnp.where(left, v[1], pltpu.roll(v[3], 64, 1))
                w3 = jnp.where(left, pltpu.roll(v[1], 64, 1), v[3])
                even = jnp.bitwise_and(lane, 32) == 0
                blocks = [
                    jnp.where(even, w0, pltpu.roll(w1, 32, 1)),
                    jnp.where(even, pltpu.roll(w0, 96, 1), w1),
                    jnp.where(even, w2, pltpu.roll(w3, 32, 1)),
                    jnp.where(even, pltpu.roll(w2, 96, 1), w3),
                ]
                for b in range(4):
                    spot = (step * SWAP + n) * 8 + c * 4 + b
                    out[spot] = blocks[b].astype(jnp.bfloat16)
        return carry

    lax.fori_loop(0, tiles // SWAP, swap, 0)


def finish_kernel(
    freq_blocks, offsets, strength, wind_speed, wind_dir, blocks, out, table, relaid, rows
):
    nblocks, _, _ = blocks.shape
    pairs = nblocks // freq_blocks
    reach = DSPAN // 2
    freqs = NFREQ // freq_blocks
    low_pad = 8
    lane = lax.broadcasted_iota(jnp.int32, (NFREQ, LANES), 1)
    first = lane < 32
    half = lane < 64
    ndirs = 2 * pairs
    npts = 32

    edge = jnp.zeros((8, LANES), jnp.float32)
    for parity in range(2):
        for s in range(pairs + 2 * reach):
            table[parity, s, 0:8] = edge
            table[parity, s, low_pad + NFREQ : low_pad + NFREQ + 8] = edge

    def unpack(s, carry):
        for b in range(freq_blocks):
            piece = blocks[s * freq_blocks + b].astype(jnp.float32)
            table[0, s + reach, low_pad + b * freqs : low_pad + (b + 1) * freqs] = piece[:freqs]
        body = table[0, s + reach, low_pad : low_pad + NFREQ]
        turned = jnp.where(first, pltpu.roll(body, LANES - 32, 1), pltpu.roll(body, 32, 1))
        table[1, s + reach, low_pad : low_pad + NFREQ] = turned
        return carry

    lax.fori_loop(0, pairs, unpack, 0)
    for parity in range(2):
        for s in range(reach):
            table[parity, s] = table[parity, s + pairs]
            table[parity, s + pairs + reach] = table[parity, s + reach]

    def transfer(s, carry):
        total = carry
        body = table[0, s + reach, low_pad : low_pad + NFREQ]
        moved = body + pltpu.roll(body, 64, 1)
        change = jnp.zeros((NFREQ, LANES), jnp.float32)
        for q in range(strength.shape[0]):
            d = offsets[0, q]
            m = offsets[1, q]
            odd = jnp.bitwise_and(d, 1)

            def shifted(by, start):
                near = s + reach + jnp.right_shift(by, 1)
                far = s + reach + jnp.right_shift(by + 1, 1)
                at = pl.ds(low_pad + start, NFREQ)
                return jnp.where(first, table[odd, near, at], table[odd, far, at])

            upper = shifted(d, m)
            lower = shifted(-d, -m)
            delta = body * body * (upper + lower) - 2.0 * body * upper * lower
            change = change + strength[q] * delta
        value = moved + DT_NL * change
        relaid[s] = value
        return total + value

    total = lax.fori_loop(0, pairs, transfer, jnp.zeros((NFREQ, LANES), jnp.float32))

    sigma = sigma_of(lax.broadcasted_iota(jnp.int32, (NFREQ, LANES), 0))
    weight = 1.0 / (ndirs * NFREQ)

    def over_dirs(x):
        x = jnp.sum(x, axis=0, keepdims=True)
        x = jnp.broadcast_to(x, (8, LANES))
        lane8 = lane[:8]
        x = x + jnp.where(lane8 < 32, pltpu.roll(x, LANES - 32, 1), pltpu.roll(x, 32, 1))
        return x[:1]

    etot = over_dirs(total) * weight
    inverse = over_dirs(total / sigma) * weight
    msig = jnp.clip(etot / jnp.maximum(inverse, INV_FLOOR), SIG_LO, SIG_HI)
    steep = etot * (msig * msig * msig * msig) / APM
    ratio = sigma / msig
    rate = CDS * (ratio * ratio) * msig * (steep * steep)
    damp = 1.0 / (1.0 + rate)
    wind = jnp.concatenate([wind_speed[...]] * 4, axis=1) * sigma
    towards = jnp.concatenate([wind_dir[...]] * 4, axis=1)
    step = lax.broadcasted_iota(jnp.int32, (pairs, LANES), 0) * 2 + jnp.bitwise_and(
        jnp.right_shift(lax.broadcasted_iota(jnp.int32, (pairs, LANES), 1), 5), 1
    )
    rows[...] = jnp.cos((2.0 * math.pi / ndirs) * step.astype(jnp.float32) - towards)
    push = BETA * sigma

    def grow(s, carry):
        growth = push * jnp.maximum(wind * rows[pl.ds(s, 1), :] - 1.0, 0.0)
        value = relaid[s] * (1.0 + growth) * damp
        out[s] = value[:, :64]
        return carry

    lax.fori_loop(0, pairs, grow, 0)


def local_scoped(ndirs, *refs):
    freqs, dirs, npoints = refs[0].shape
    sums = [
        pltpu.ACC(unit)((3 * npoints // TILE, TILE), jnp.float32)
        for unit in range(2)
        for _ in range(2 * dirs * freqs // 3)
    ]
    pl.run_scoped(lambda *sums: local_kernel(ndirs, *refs, *sums), *sums)


def local_call(
    ndirs, parts, spectrum, neighbours, edge_angle, edge_coef, land_mask, space_order
):
    dirs, freqs, npoints = spectrum.shape
    tiles = npoints // TILE
    near = neighbours.shape[0]
    vmem = pl.BlockSpec(memory_space=pltpu.VMEM)
    return pl.pallas_call(
        functools.partial(local_scoped, ndirs),
        out_shape=jax.ShapeDtypeStruct((parts, 8, LANES), jnp.bfloat16),
        in_specs=[pl.BlockSpec(memory_space=pltpu.MemorySpace.HBM)] * 6,
        out_specs=vmem,
        scratch_shapes=[
            pltpu.VMEM((freqs, dirs, npoints), jnp.float32),
            pltpu.VMEM((near, npoints), jnp.int32),
            pltpu.VMEM((near, npoints), jnp.float32),
            pltpu.VMEM((near, npoints), jnp.float32),
            pltpu.VMEM((1, npoints), jnp.int32),
            pltpu.VMEM((1, npoints), jnp.int32),
            pltpu.SemaphoreType.DMA((6,)),
            pltpu.VMEM((dirs, 8, npoints), jnp.float32),
            pltpu.VMEM((TILE // LANES, dirs * freqs * tiles, LANES), jnp.float32),
            pltpu.VMEM((dirs * freqs * tiles, TILE), jnp.bfloat16),
            pltpu.VMEM((2 * dirs * freqs * tiles, TILE), jnp.float32),
            pltpu.VMEM((2 * dirs * freqs * tiles, TILE), jnp.bfloat16),
            pltpu.VMEM((TILE, TILE), jnp.bfloat16),
        ],
        compiler_params=pltpu.CompilerParams(vmem_limit_bytes=40 * 1024 * 1024),
        name="local_step",
    )(
        *(
            pltpu.with_memory_space_constraint(x, pltpu.MemorySpace.HBM)
            for x in (
                spectrum.transpose(1, 0, 2),
                neighbours,
                edge_angle,
                edge_coef,
                land_mask.reshape(1, npoints),
                space_order.reshape(1, npoints),
            )
        )
    )


def on_device(
    spectrum,
    neighbours,
    edge_angle,
    edge_coef,
    land_mask,
    dia_offsets,
    dia_coef,
    space_order,
    wind_speed,
    wind_dir,
):
    dirs, freqs, npoints = spectrum.shape
    nd, nf = lax.axis_size("dir"), lax.axis_size("freq")
    parts = nd * nf
    vmem = pl.BlockSpec(memory_space=pltpu.VMEM)
    smem = pl.BlockSpec(memory_space=pltpu.SMEM)
    blocks = local_call(
        nd * dirs, parts, spectrum, neighbours, edge_angle, edge_coef, land_mask, space_order
    )
    blocks = lax.all_to_all(blocks, ("dir", "freq"), split_axis=0, concat_axis=0, tiled=True)
    npts = npoints // parts
    done = pl.pallas_call(
        functools.partial(finish_kernel, nf),
        out_shape=jax.ShapeDtypeStruct((nd, NFREQ, 2 * npts), jnp.float32),
        in_specs=[smem, smem, vmem, vmem, vmem],
        out_specs=vmem,
        scratch_shapes=[
            pltpu.VMEM((2, nd + DSPAN, NFREQ + 16, LANES), jnp.float32),
            pltpu.VMEM((nd, NFREQ, LANES), jnp.float32),
            pltpu.VMEM((nd, LANES), jnp.float32),
        ],
        compiler_params=pltpu.CompilerParams(vmem_limit_bytes=40 * 1024 * 1024),
        name="finish_step",
    )(dia_offsets, dia_coef, wind_speed.reshape(1, npts), wind_dir.reshape(1, npts), blocks)
    done = done.reshape(nd, NFREQ, 2, npts).transpose(0, 2, 1, 3)
    return done.reshape(2 * nd, NFREQ, npts)


def solution(mesh):
    in_specs = (
        P("dir", "freq", None),
        P(),
        P(),
        P(),
        P(),
        P(),
        P(),
        P(),
        P(("dir", "freq")),
        P(("dir", "freq")),
    )
    out_specs = P(None, None, ("dir", "freq"))
    return jax.shard_map(
        on_device, mesh=mesh, in_specs=in_specs, out_specs=out_specs, check_vma=False
    )
```

```python
import functools
import math

import jax
import jax.numpy as jnp
from jax import lax
from jax.experimental import pallas as pl
from jax.experimental.pallas import tpu as pltpu
from jax.sharding import PartitionSpec as P

NFREQ = 48
DSPAN = 6
FSPAN = 2

SIG_LO = 0.35
SIG_HI = 2.8
DT_NL = 0.1
CDS = 0.05
APM = 0.4
BETA = 0.05
INV_FLOOR = 0.01

LANES = 128
TILE = 256
WIDEN, UNPACK, TRANSFER, GROW = 8, 8, 4, 8
STAGE, ADVECT, SWAP = 2, 8, 8
CENTRE = 0.5


def sigma_of(index):
    return SIG_LO * jnp.exp(index.astype(jnp.float32) * (math.log(SIG_HI / SIG_LO) / (NFREQ - 1)))


def one_hot(low, ramp):
    one, none = jnp.ones((), jnp.bfloat16), jnp.zeros((), jnp.bfloat16)
    return jnp.where(ramp == low.astype(jnp.float32).astype(jnp.bfloat16), one, none)


def local_kernel(
    ndirs, spec_at, nbr_at, angle_at, coef_at, mask_at, order_at, out,
    spec, nbr, angle, coef, mask, order, arrived, field, pickf, pick, keepf, keep, ramp, *sums
):
    freqs, dirs, npoints = spec.shape
    tiles = npoints // TILE
    near = nbr.shape[0]
    first_dir = lax.axis_index("dir") * dirs
    first_freq = lax.axis_index("freq") * freqs
    pairs = [(spec_at, spec), (mask_at, mask), (nbr_at, nbr)]
    pairs += [(angle_at, angle), (coef_at, coef), (order_at, order)]
    copies = [
        pltpu.make_async_copy(src, dst, arrived.at[n]) for n, (src, dst) in enumerate(pairs)
    ]
    for copy in copies:
        copy.start()
    sub = lax.broadcasted_iota(jnp.int32, (8, TILE), 0)
    lane = lax.broadcasted_iota(jnp.int32, (8, LANES), 1)
    speed = 0.5 / sigma_of(first_freq + sub)
    ramp[...] = lax.broadcasted_iota(jnp.int32, (TILE, TILE), 0).astype(jnp.float32).astype(jnp.bfloat16)
    pad = jnp.zeros((8 - freqs, TILE), jnp.float32)
    for copy in copies[:2]:
        copy.wait()

    def span(t):
        return pl.ds(pl.multiple_of(t * TILE, TILE), TILE)

    def stage(t, carry):
        at = span(t)
        wet_row = mask[:, at].astype(jnp.float32)
        for i in range(dirs):
            rows = [spec[f, pl.ds(i, 1), at] for f in range(freqs)]
            value = jnp.concatenate(rows + [pad], axis=0)
            field[i, :, at] = value
            shown = value * wet_row - CENTRE
            spot = pl.ds(i * freqs * tiles + t, freqs, stride=tiles)
            for c in range(TILE // LANES):
                pickf[c, spot, :] = shown[:freqs, c * LANES : (c + 1) * LANES]
        return carry

    lax.fori_loop(0, tiles, stage, 0, unroll=STAGE)
    for c in range(TILE // LANES):
        pick[:, c * LANES : (c + 1) * LANES] = pickf[c].astype(jnp.bfloat16)
    for copy in copies[2:5]:
        copy.wait()

    def split(index):
        low = jnp.bitwise_and(index, TILE - 1)
        high = jnp.broadcast_to(jnp.right_shift(index, 8), (8, TILE))
        return one_hot(low, ramp[...]), high

    def issue(job, table, accs, index, chunk):
        unit, slot = job % 2, job // 2 % 2
        hot, high = split(index)
        pltpu.matmul_push_rhs(hot, slot, unit)
        for c, acc in enumerate(accs[unit][slot]):
            rows = table[c * chunk : (c + 1) * chunk, :]
            pltpu.matmul_acc_lhs(acc, rows, load_staged_rhs=slot if c == 0 else None)
        return high

    groups = tiles // 8
    chunk = 3 * tiles
    width = 2 * dirs * freqs
    count = dirs * freqs // 3
    accs = [[sums[(u * 2 + v) * count : (u * 2 + v + 1) * count] for v in range(2)] for u in range(2)]

    def advect(step, carry):
        jobs = [(u, k) for u in range(ADVECT) for k in range(near)]
        highs = {}

        def start(n):
            u, k = jobs[n]
            highs[n] = issue(n, pick, accs, nbr[k : k + 1, span(step * ADVECT + u)], chunk)

        start(0)
        start(1)
        for n, (u, k) in enumerate(jobs):
            t = step * ADVECT + u
            at = span(t)
            if k == 0:
                total = [jnp.zeros((8, TILE), jnp.float32) for _ in range(dirs * freqs)]
                geom = []
                for i in range(dirs):
                    theta = (2.0 * math.pi / ndirs) * (first_dir + i).astype(jnp.float32)
                    bearing = jnp.cos(theta - angle[:, at])
                    geom.append(coef[:, at] * jnp.maximum(bearing, 0.0))
            high = highs.pop(n)
            match = [high == sub + 8 * h for h in range(groups)]
            rows = [geom[i][k : k + 1] for i in range(dirs)]
            unit, slot = n % 2, n // 2 % 2
            for c, acc in enumerate(accs[unit][slot]):
                found = pltpu.matmul_pop(acc)
                for x in range(3):
                    r = c * 3 + x
                    chosen = jnp.zeros((8, TILE), jnp.float32)
                    for h in range(groups):
                        begin = x * tiles + 8 * h
                        chosen = jnp.where(match[h], found[begin : begin + 8], chosen)
                    total[r] = total[r] + rows[r // freqs] * chosen
            if n + 2 < len(jobs):
                start(n + 2)
            if k == near - 1:
                wet_row = mask[:, at].astype(jnp.float32)
                for i in range(dirs):
                    value = field[i, :, at]
                    weight = jnp.sum(geom[i], axis=0, keepdims=True)
                    lines = [
                        jnp.sum(total[i * freqs + f], axis=0, keepdims=True) for f in range(freqs)
                    ]
                    inflow = jnp.concatenate(lines + [pad], axis=0)
                    moved = value + speed * (inflow + weight * (CENTRE - value))
                    old = value.astype(jnp.bfloat16).astype(jnp.float32)
                    for n, part in enumerate((wet_row * old, wet_row * (moved - old))):
                        spot = pl.ds(t * width + i * 2 + n, freqs, stride=2 * dirs)
                        for c in range(TILE // LANES):
                            keepf[c, spot, :] = part[:freqs, c * LANES : (c + 1) * LANES]
        return carry

    lax.fori_loop(0, tiles // ADVECT, advect, 0)
    for c in range(TILE // LANES):
        keep[:, c * LANES : (c + 1) * LANES] = keepf[c].astype(jnp.bfloat16)
    copies[5].wait()

    row = sub[:, :LANES]
    outer = jnp.right_shift(row, 2) == jnp.right_shift(lane, 6)
    inner = jnp.bitwise_and(row, 2) == jnp.bitwise_and(jnp.right_shift(lane, 4), 2)
    first = jnp.bitwise_and(row, 2) == 0

    def swap(step, carry):
        jobs = list(range(SWAP))
        highs = {}
        hots = {}
        accs = [[*sums[: 2 * count]], [*sums[2 * count :]]]

        def push(n):
            hots[n], highs[n] = split(order[:, span(step * SWAP + n)])
            pltpu.matmul_push_rhs(hots[n], n // 2 % 2, n % 2)

        def multiply(n, c):
            rows = keep[c * chunk : (c + 1) * chunk, :]
            slot = n // 2 % 2 if c == 0 else None
            pltpu.matmul_acc_lhs(accs[n % 2][c], rows, load_staged_rhs=slot)

        for n in jobs[:2]:
            push(n)
            for c in range(2 * count):
                multiply(n, c)
        for n in jobs:
            high = highs.pop(n)
            part = [jnp.zeros((8, TILE), jnp.float32) for _ in range(width // 8)]
            if n + 2 < len(jobs):
                push(n + 2)
            for c in range(2 * count):
                found = pltpu.matmul_pop(accs[n % 2][c])
                if n + 2 < len(jobs):
                    multiply(n + 2, c)
                for x in range(chunk // width):
                    match = high == c * (chunk // width) + x
                    for g in range(width // 8):
                        begin = x * width + 8 * g
                        part[g] = jnp.where(match, found[begin : begin + 8], part[g])
            for g, whole in enumerate(part):
                for c in range(TILE // LANES):
                    x = whole[:, c * LANES : (c + 1) * LANES]
                    x = jnp.where(outer, x, pltpu.roll(pltpu.roll(x, 4, 0), 64, 1))
                    after = pltpu.roll(pltpu.roll(x, 6, 0), 32, 1)
                    before = pltpu.roll(pltpu.roll(x, 2, 0), 96, 1)
                    x = jnp.where(inner, x, jnp.where(first, after, before)).astype(jnp.bfloat16)
                    for b in range(4):
                        spot = ((step * SWAP + n) * 8 + c * 4 + b) * (width // 8) + g
                        out[spot] = x[2 * b : 2 * b + 2]
        return carry

    lax.fori_loop(0, tiles // SWAP, swap, 0)


def finish_kernel(
    ndirs, offsets, strength, wind_speed, wind_dir, blocks, out, table, relaid, rows, lines
):
    pairs = ndirs // 2
    reach = DSPAN // 2
    lots = table.shape[2] - 2
    sub = lax.broadcasted_iota(jnp.int32, (8, LANES), 0)
    lane = lax.broadcasted_iota(jnp.int32, (8, LANES), 1)
    second = jnp.bitwise_and(lane, 32) == 0
    first = lane < 64
    per = 8 * lots

    def turn(x):
        return jnp.where(second, pltpu.roll(x, LANES - 32, 1), pltpu.roll(x, 32, 1))

    def widen(s, carry):
        piece = blocks[pl.ds(s * per, per)].astype(jnp.float32)
        spot = pl.ds(pl.multiple_of(s * 2 * per, 2 * per), 2 * per)
        lines[spot, :] = piece.reshape(2 * per, LANES)
        return carry

    lax.fori_loop(0, pairs, widen, 0, unroll=WIDEN)

    def unpack(s, carry):
        for b in range(lots):
            begin = s * 2 * per + 2 * b
            old = lines[pl.ds(begin, 8, stride=2 * lots), :]
            relaid[b, s] = lines[pl.ds(begin + 1, 8, stride=2 * lots), :]
            other = pltpu.roll(old, 64, 1)
            forms = ((old, turn(old)), (other, turn(other)))
            for i in range(2):
                for j in range(2):
                    table[i, j, b + 1, s + reach] = forms[i][j]
                    if b == 0:
                        shifted = jnp.where(sub == 7, 0.0, pltpu.roll(forms[i][j], 7, 0))
                        table[i, j, lots + 1, s + reach] = shifted
                    if b == lots - 1:
                        shifted = jnp.where(sub == 0, 0.0, pltpu.roll(forms[i][j], 1, 0))
                        table[i, j, 0, s + reach] = shifted
        return carry

    lax.fori_loop(0, pairs, unpack, 0, unroll=UNPACK)
    for i in range(2):
        for j in range(2):
            for b in range(lots + 2):
                for s in range(reach):
                    table[i, j, b, s] = table[i, j, b, s + pairs]
                    table[i, j, b, s + pairs + reach] = table[i, j, b, s + reach]

    shapes = []
    for q in range(strength.shape[0]):
        d, m, c = offsets[0, q], offsets[1, q], strength[q]
        at = [jnp.right_shift(m + x, 1) + 1 for x in range(2)]
        to = [jnp.right_shift(d + x, 1) + reach for x in range(2)]
        back_at = [jnp.right_shift(x - m, 1) + 1 for x in range(2)]
        back_to = [jnp.right_shift(x - d, 1) + reach for x in range(2)]
        odd = (jnp.bitwise_and(m, 1), jnp.bitwise_and(d, 1))
        shapes.append((odd, at, to, back_at, back_to, c))

    def transfer(s, carry):
        total = list(carry)
        for b in range(lots):
            body = table[0, 0, b + 1, s + reach]
            plain = jnp.zeros((8, LANES), jnp.float32)
            cross = jnp.zeros((8, LANES), jnp.float32)
            for odd, at, to, back_at, back_to, c in shapes:

                def shifted(at, to):
                    got = [[table[odd[0], odd[1], b + x, s + y] for y in to] for x in at]
                    got = [jnp.where(second, x[0], x[1]) for x in got]
                    return jnp.where(first, got[0], got[1])

                upper, lower = shifted(at, to), shifted(back_at, back_to)
                plain = plain + c * (upper + lower)
                cross = cross + (2.0 * c) * (upper * lower)
            value = body + relaid[b, s] + DT_NL * (body * (body * plain - cross))
            relaid[b, s] = value
            total[b] = total[b] + value
        return tuple(total)

    empty = jnp.zeros((8, LANES), jnp.float32)
    total = lax.fori_loop(0, pairs, transfer, (empty,) * lots, unroll=TRANSFER)

    half = jnp.right_shift(lane, 6)
    sigma = [sigma_of(sub * (2 * lots) + 2 * b + half) for b in range(lots)]
    weight = 1.0 / (ndirs * NFREQ)

    def over_all(terms):
        x = jnp.sum(sum(terms), axis=0, keepdims=True)
        x = jnp.broadcast_to(x, (8, LANES))
        x = x + pltpu.roll(x, 64, 1)
        return x + pltpu.roll(x, 32, 1)

    etot = over_all(total) * weight
    inverse = over_all([x / y for x, y in zip(total, sigma)]) * weight
    msig = jnp.clip(etot / jnp.maximum(inverse, INV_FLOOR), SIG_LO, SIG_HI)
    steep = etot * (msig * msig * msig * msig) / APM
    rate = [CDS * ((x / msig) * (x / msig)) * msig * (steep * steep) for x in sigma]
    damp = [1.0 / (1.0 + x) for x in rate]
    speed = jnp.concatenate([wind_speed[...]] * 4, axis=1)
    wind = [speed * x for x in sigma]
    push = [BETA * x for x in sigma]
    towards = jnp.concatenate([wind_dir[...]] * 4, axis=1)
    step = lax.broadcasted_iota(jnp.int32, (pairs, LANES), 0) * 2 + jnp.bitwise_and(
        jnp.right_shift(lax.broadcasted_iota(jnp.int32, (pairs, LANES), 1), 5), 1
    )
    rows[...] = jnp.cos((2.0 * math.pi / ndirs) * step.astype(jnp.float32) - towards)

    def grow(s, carry):
        along = rows[pl.ds(s, 1), :]
        for b in range(lots):
            growth = push[b] * jnp.maximum(wind[b] * along - 1.0, 0.0)
            value = relaid[b, s] * (1.0 + growth) * damp[b]
            out[s, pl.ds(2 * b, 8, stride=2 * lots), :] = value
            out[s, pl.ds(2 * b + 1, 8, stride=2 * lots), :] = pltpu.roll(value, 64, 1)
        return carry

    lax.fori_loop(0, pairs, grow, 0, unroll=GROW)


def local_scoped(ndirs, *refs):
    freqs, dirs, npoints = refs[0].shape
    sums = [
        pltpu.ACC(unit)((3 * npoints // TILE, TILE), jnp.float32)
        for unit in range(2)
        for _ in range(2 * dirs * freqs // 3)
    ]
    pl.run_scoped(lambda *sums: local_kernel(ndirs, *refs, *sums), *sums)


def local_call(
    ndirs, parts, spectrum, neighbours, edge_angle, edge_coef, land_mask, space_order
):
    dirs, freqs, npoints = spectrum.shape
    tiles = npoints // TILE
    near = neighbours.shape[0]
    vmem = pl.BlockSpec(memory_space=pltpu.VMEM)
    return pl.pallas_call(
        functools.partial(local_scoped, ndirs),
        out_shape=jax.ShapeDtypeStruct((parts * dirs * freqs // 4, 2, LANES), jnp.bfloat16),
        in_specs=[pl.BlockSpec(memory_space=pltpu.MemorySpace.HBM)] * 6,
        out_specs=vmem,
        scratch_shapes=[
            pltpu.VMEM((freqs, dirs, npoints), jnp.float32),
            pltpu.VMEM((near, npoints), jnp.int32),
            pltpu.VMEM((near, npoints), jnp.float32),
            pltpu.VMEM((near, npoints), jnp.float32),
            pltpu.VMEM((1, npoints), jnp.int32),
            pltpu.VMEM((1, npoints), jnp.int32),
            pltpu.SemaphoreType.DMA((6,)),
            pltpu.VMEM((dirs, 8, npoints), jnp.float32),
            pltpu.VMEM((TILE // LANES, dirs * freqs * tiles, LANES), jnp.float32),
            pltpu.VMEM((dirs * freqs * tiles, TILE), jnp.bfloat16),
            pltpu.VMEM((TILE // LANES, 2 * dirs * freqs * tiles, LANES), jnp.float32),
            pltpu.VMEM((2 * dirs * freqs * tiles, TILE), jnp.bfloat16),
            pltpu.VMEM((TILE, TILE), jnp.bfloat16),
        ],
        compiler_params=pltpu.CompilerParams(vmem_limit_bytes=40 * 1024 * 1024),
        name="local_step",
    )(
        *(
            pltpu.with_memory_space_constraint(x, pltpu.MemorySpace.HBM)
            for x in (
                spectrum.transpose(1, 0, 2),
                neighbours,
                edge_angle,
                edge_coef,
                land_mask.reshape(1, npoints),
                space_order.reshape(1, npoints),
            )
        )
    )


def finish_call(ndirs, nd, nf, dia_offsets, dia_coef, wind_speed, wind_dir, blocks):
    vmem = pl.BlockSpec(memory_space=pltpu.VMEM)
    smem = pl.BlockSpec(memory_space=pltpu.SMEM)
    lots = blocks.shape[0] // (nd * nf)
    return pl.pallas_call(
        functools.partial(finish_kernel, ndirs),
        out_shape=jax.ShapeDtypeStruct((nd, NFREQ, LANES), jnp.float32),
        in_specs=[smem, smem, vmem, vmem, vmem],
        out_specs=vmem,
        scratch_shapes=[
            pltpu.VMEM((2, 2, lots + 2, nd + DSPAN, nf, LANES), jnp.float32),
            pltpu.VMEM((lots, nd, nf, LANES), jnp.float32),
            pltpu.VMEM((nd, LANES), jnp.float32),
            pltpu.VMEM((2 * nf * lots * nd, LANES), jnp.float32),
        ],
        compiler_params=pltpu.CompilerParams(vmem_limit_bytes=40 * 1024 * 1024),
        name="finish_step",
    )(dia_offsets, dia_coef, wind_speed, wind_dir, blocks)


def on_device(
    spectrum,
    neighbours,
    edge_angle,
    edge_coef,
    land_mask,
    dia_offsets,
    dia_coef,
    space_order,
    wind_speed,
    wind_dir,
):
    dirs, freqs, npoints = spectrum.shape
    nd, nf = lax.axis_size("dir"), lax.axis_size("freq")
    parts = nd * nf
    blocks = local_call(
        nd * dirs, parts, spectrum, neighbours, edge_angle, edge_coef, land_mask, space_order
    )
    blocks = lax.all_to_all(blocks, ("dir", "freq"), split_axis=0, concat_axis=0, tiled=True)
    npts = npoints // parts
    done = finish_call(
        nd * dirs, nd, nf, dia_offsets, dia_coef,
        wind_speed.reshape(1, npts), wind_dir.reshape(1, npts), blocks,
    )
    done = done[:, :, : 2 * npts].reshape(nd, NFREQ, 2, npts).transpose(0, 2, 1, 3)
    return done.reshape(2 * nd, NFREQ, npts)


def solution(mesh):
    in_specs = (
        P("dir", "freq", None),
        P(),
        P(),
        P(),
        P(),
        P(),
        P(),
        P(),
        P(("dir", "freq")),
        P(("dir", "freq")),
    )
    out_specs = P(None, None, ("dir", "freq"))
    return jax.shard_map(
        on_device, mesh=mesh, in_specs=in_specs, out_specs=out_specs, check_vma=False
    )
```

```python
import functools
import math

import jax
import jax.numpy as jnp
from jax import lax
from jax.experimental import pallas as pl
from jax.experimental.pallas import tpu as pltpu
from jax.sharding import PartitionSpec as P

NFREQ = 48
DSPAN = 6
FSPAN = 2

SIG_LO = 0.35
SIG_HI = 2.8
DT_NL = 0.1
CDS = 0.05
APM = 0.4
BETA = 0.05
INV_FLOOR = 0.01

LANES = 128
TILE = 256
WIDEN, UNPACK, TRANSFER, GROW, PLACE = 8, 8, 4, 8, 4
STAGE, ADVECT, SWAP = 4, 8, 16
ROUND = 1.5 * 2.0**23
SINE = (1.0, -0.16666667, 0.008333329, -0.00019840701, 2.7518759e-06, -2.3793149e-08)
CENTRE = 0.5


def sigma_of(index):
    return SIG_LO * jnp.exp(index.astype(jnp.float32) * (math.log(SIG_HI / SIG_LO) / (NFREQ - 1)))


def cosine(x):
    turns = (x * (0.5 / math.pi) + ROUND) - ROUND
    h = (x * 0.5 - turns * 3.140625) - turns * (math.pi - 3.140625)
    z = h * h
    p = SINE[-1]
    for c in SINE[-2::-1]:
        p = p * z + c
    s = p * h
    return 1.0 - 2.0 * (s * s)


def one_hot(low, ramp):
    one, none = jnp.ones((), jnp.bfloat16), jnp.zeros((), jnp.bfloat16)
    return jnp.where(ramp == low.astype(jnp.float32).astype(jnp.bfloat16), one, none)


def local_kernel(
    ndirs, spec_at, nbr_at, angle_at, coef_at, mask_at, order_at, out,
    spec, nbr, angle, coef, mask, order, arrived, field, pickf, pick, keepf, keep, ramp, *sums
):
    freqs, dirs, npoints = spec.shape
    tiles = npoints // TILE
    near = nbr.shape[0]
    first_dir = lax.axis_index("dir") * dirs
    first_freq = lax.axis_index("freq") * freqs
    pairs = [(spec_at, spec), (mask_at, mask), (nbr_at, nbr)]
    pairs += [(angle_at, angle), (coef_at, coef), (order_at, order)]
    copies = [
        pltpu.make_async_copy(src, dst, arrived.at[n]) for n, (src, dst) in enumerate(pairs)
    ]
    for copy in copies:
        copy.start()
    sub = lax.broadcasted_iota(jnp.int32, (8, TILE), 0)
    lane = lax.broadcasted_iota(jnp.int32, (8, LANES), 1)
    speed = 0.5 / sigma_of(first_freq + sub)
    ramp[...] = lax.broadcasted_iota(jnp.int32, (TILE, TILE), 0).astype(jnp.float32).astype(jnp.bfloat16)
    pad = jnp.zeros((8 - freqs, TILE), jnp.float32)
    for copy in copies[:2]:
        copy.wait()

    def span(t):
        return pl.ds(pl.multiple_of(t * TILE, TILE), TILE)

    def stage(t, carry):
        at = span(t)
        wet_row = mask[:, at].astype(jnp.float32)
        for i in range(dirs):
            rows = [spec[f, pl.ds(i, 1), at] for f in range(freqs)]
            value = jnp.concatenate(rows + [pad], axis=0)
            field[i, :, at] = value
            shown = value * wet_row - CENTRE
            spot = pl.ds(i * freqs * tiles + t, freqs, stride=tiles)
            for c in range(TILE // LANES):
                pickf[c, spot, :] = shown[:freqs, c * LANES : (c + 1) * LANES]
        return carry

    lax.fori_loop(0, tiles, stage, 0, unroll=STAGE)
    for c in range(TILE // LANES):
        pick[:, c * LANES : (c + 1) * LANES] = pickf[c].astype(jnp.bfloat16)
    for copy in copies[2:5]:
        copy.wait()

    def split(index):
        low = jnp.bitwise_and(index, TILE - 1)
        high = jnp.broadcast_to(jnp.right_shift(index, 8), (8, TILE))
        return one_hot(low, ramp[...]), high

    def issue(job, table, accs, index, chunk):
        unit, slot = job % 2, job // 2 % 2
        hot, high = split(index)
        pltpu.matmul_push_rhs(hot, slot, unit)
        for c, acc in enumerate(accs[unit][slot]):
            rows = table[c * chunk : (c + 1) * chunk, :]
            pltpu.matmul_acc_lhs(acc, rows, load_staged_rhs=slot if c == 0 else None)
        return high

    groups = tiles // 8
    chunk = 3 * tiles
    width = 2 * dirs * freqs
    count = dirs * freqs // 3
    accs = [[sums[(u * 2 + v) * count : (u * 2 + v + 1) * count] for v in range(2)] for u in range(2)]

    def advect(step, carry):
        jobs = [(u, k) for u in range(ADVECT) for k in range(near)]
        highs = {}

        def start(n):
            u, k = jobs[n]
            highs[n] = issue(n, pick, accs, nbr[k : k + 1, span(step * ADVECT + u)], chunk)

        start(0)
        start(1)
        for n, (u, k) in enumerate(jobs):
            t = step * ADVECT + u
            at = span(t)
            if k == 0:
                total = [jnp.zeros((8, TILE), jnp.float32) for _ in range(dirs * freqs)]
                geom = []
                for i in range(dirs):
                    theta = (2.0 * math.pi / ndirs) * (first_dir + i).astype(jnp.float32)
                    bearing = cosine(theta - angle[:, at])
                    geom.append(coef[:, at] * jnp.maximum(bearing, 0.0))
            high = highs.pop(n)
            match = [high == sub + 8 * h for h in range(groups)]
            rows = [geom[i][k : k + 1] for i in range(dirs)]
            unit, slot = n % 2, n // 2 % 2
            for c, acc in enumerate(accs[unit][slot]):
                found = pltpu.matmul_pop(acc)
                for x in range(3):
                    r = c * 3 + x
                    chosen = jnp.zeros((8, TILE), jnp.float32)
                    for h in range(groups):
                        begin = x * tiles + 8 * h
                        chosen = jnp.where(match[h], found[begin : begin + 8], chosen)
                    total[r] = total[r] + rows[r // freqs] * chosen
            if n + 2 < len(jobs):
                start(n + 2)
            if k == near - 1:
                wet_row = mask[:, at].astype(jnp.float32)
                for i in range(dirs):
                    value = field[i, :, at]
                    weight = jnp.sum(geom[i], axis=0, keepdims=True)
                    lines = [
                        jnp.sum(total[i * freqs + f], axis=0, keepdims=True) for f in range(freqs)
                    ]
                    inflow = jnp.concatenate(lines + [pad], axis=0)
                    moved = value + speed * (inflow + weight * (CENTRE - value))
                    old = value.astype(jnp.bfloat16).astype(jnp.float32)
                    for n, part in enumerate((wet_row * old, wet_row * (moved - old))):
                        spot = pl.ds(t * width + i * 2 + n, freqs, stride=2 * dirs)
                        for c in range(TILE // LANES):
                            keepf[c, spot, :] = part[:freqs, c * LANES : (c + 1) * LANES]
        return carry

    lax.fori_loop(0, tiles // ADVECT, advect, 0)
    for c in range(TILE // LANES):
        keep[:, c * LANES : (c + 1) * LANES] = keepf[c].astype(jnp.bfloat16)
    copies[5].wait()

    row = sub[:, :LANES]
    outer = jnp.right_shift(row, 2) == jnp.right_shift(lane, 6)
    inner = jnp.bitwise_and(row, 2) == jnp.bitwise_and(jnp.right_shift(lane, 4), 2)
    first = jnp.bitwise_and(row, 2) == 0

    def swap(step, carry):
        jobs = list(range(SWAP))
        highs = {}
        hots = {}
        accs = [[*sums[: 2 * count]], [*sums[2 * count :]]]

        def push(n):
            hots[n], highs[n] = split(order[:, span(step * SWAP + n)])
            pltpu.matmul_push_rhs(hots[n], n // 2 % 2, n % 2)

        def multiply(n, c):
            rows = keep[c * chunk : (c + 1) * chunk, :]
            slot = n // 2 % 2 if c == 0 else None
            pltpu.matmul_acc_lhs(accs[n % 2][c], rows, load_staged_rhs=slot)

        for n in jobs[:2]:
            push(n)
            for c in range(2 * count):
                multiply(n, c)
        for n in jobs:
            high = highs.pop(n)
            part = [jnp.zeros((8, TILE), jnp.float32) for _ in range(width // 8)]
            if n + 2 < len(jobs):
                push(n + 2)
            for c in range(2 * count):
                found = pltpu.matmul_pop(accs[n % 2][c])
                if n + 2 < len(jobs):
                    multiply(n + 2, c)
                for x in range(chunk // width):
                    match = high == c * (chunk // width) + x
                    for g in range(width // 8):
                        begin = x * width + 8 * g
                        part[g] = jnp.where(match, found[begin : begin + 8], part[g])
            for g, whole in enumerate(part):
                for c in range(TILE // LANES):
                    x = whole[:, c * LANES : (c + 1) * LANES]
                    x = jnp.where(outer, x, pltpu.roll(pltpu.roll(x, 4, 0), 64, 1))
                    after = pltpu.roll(pltpu.roll(x, 6, 0), 32, 1)
                    before = pltpu.roll(pltpu.roll(x, 2, 0), 96, 1)
                    x = jnp.where(inner, x, jnp.where(first, after, before)).astype(jnp.bfloat16)
                    for b in range(4):
                        spot = ((step * SWAP + n) * 8 + c * 4 + b) * (width // 8) + g
                        out[spot] = x[2 * b : 2 * b + 2]
        return carry

    lax.fori_loop(0, tiles // SWAP, swap, 0)


def finish_kernel(
    ndirs, offsets, strength, wind_speed, wind_dir, blocks, out_at, table, relaid, rows, lines, turned, out, left
):
    pairs = ndirs // 2
    reach = DSPAN // 2
    lots = table.shape[2] - 2
    sub = lax.broadcasted_iota(jnp.int32, (8, LANES), 0)
    lane = lax.broadcasted_iota(jnp.int32, (8, LANES), 1)
    second = jnp.bitwise_and(lane, 32) == 0
    first = lane < 64
    per = 8 * lots

    def turn(x):
        return jnp.where(second, pltpu.roll(x, LANES - 32, 1), pltpu.roll(x, 32, 1))

    def widen(s, carry):
        piece = blocks[pl.ds(s * per, per)].astype(jnp.float32)
        spot = pl.ds(pl.multiple_of(s * 2 * per, 2 * per), 2 * per)
        lines[spot, :] = piece.reshape(2 * per, LANES)
        return carry

    lax.fori_loop(0, pairs, widen, 0, unroll=WIDEN)

    def unpack(s, carry):
        for b in range(lots):
            begin = s * 2 * per + 2 * b
            old = lines[pl.ds(begin, 8, stride=2 * lots), :]
            relaid[b, s] = lines[pl.ds(begin + 1, 8, stride=2 * lots), :]
            other = pltpu.roll(old, 64, 1)
            forms = ((old, turn(old)), (other, turn(other)))
            for i in range(2):
                for j in range(2):
                    table[i, j, b + 1, s + reach] = forms[i][j]
                    if b == 0:
                        shifted = jnp.where(sub == 7, 0.0, pltpu.roll(forms[i][j], 7, 0))
                        table[i, j, lots + 1, s + reach] = shifted
                    if b == lots - 1:
                        shifted = jnp.where(sub == 0, 0.0, pltpu.roll(forms[i][j], 1, 0))
                        table[i, j, 0, s + reach] = shifted
        return carry

    lax.fori_loop(0, pairs, unpack, 0, unroll=UNPACK)
    for i in range(2):
        for j in range(2):
            for b in range(lots + 2):
                for s in range(reach):
                    table[i, j, b, s] = table[i, j, b, s + pairs]
                    table[i, j, b, s + pairs + reach] = table[i, j, b, s + reach]

    shapes = []
    for q in range(strength.shape[0]):
        d, m, c = offsets[0, q], offsets[1, q], strength[q]
        at = [jnp.right_shift(m + x, 1) + 1 for x in range(2)]
        to = [jnp.right_shift(d + x, 1) + reach for x in range(2)]
        back_at = [jnp.right_shift(x - m, 1) + 1 for x in range(2)]
        back_to = [jnp.right_shift(x - d, 1) + reach for x in range(2)]
        odd = (jnp.bitwise_and(m, 1), jnp.bitwise_and(d, 1))
        shapes.append((odd, at, to, back_at, back_to, c))

    def transfer(s, carry):
        total = list(carry)
        for b in range(lots):
            body = table[0, 0, b + 1, s + reach]
            plain = jnp.zeros((8, LANES), jnp.float32)
            cross = jnp.zeros((8, LANES), jnp.float32)
            for odd, at, to, back_at, back_to, c in shapes:

                def shifted(at, to):
                    got = [[table[odd[0], odd[1], b + x, s + y] for y in to] for x in at]
                    got = [jnp.where(second, x[0], x[1]) for x in got]
                    return jnp.where(first, got[0], got[1])

                upper, lower = shifted(at, to), shifted(back_at, back_to)
                plain = plain + c * (upper + lower)
                cross = cross + (2.0 * c) * (upper * lower)
            value = body + relaid[b, s] + DT_NL * (body * (body * plain - cross))
            relaid[b, s] = value
            total[b] = total[b] + value
        return tuple(total)

    empty = jnp.zeros((8, LANES), jnp.float32)
    total = lax.fori_loop(0, pairs, transfer, (empty,) * lots, unroll=TRANSFER)

    half = jnp.right_shift(lane, 6)
    sigma = [sigma_of(sub * (2 * lots) + 2 * b + half) for b in range(lots)]
    weight = 1.0 / (ndirs * NFREQ)

    def over_all(terms):
        x = jnp.sum(sum(terms), axis=0, keepdims=True)
        x = jnp.broadcast_to(x, (8, LANES))
        x = x + pltpu.roll(x, 64, 1)
        return x + pltpu.roll(x, 32, 1)

    etot = over_all(total) * weight
    inverse = over_all([x / y for x, y in zip(total, sigma)]) * weight
    msig = jnp.clip(etot / jnp.maximum(inverse, INV_FLOOR), SIG_LO, SIG_HI)
    steep = etot * (msig * msig * msig * msig) / APM
    rate = [CDS * ((x / msig) * (x / msig)) * msig * (steep * steep) for x in sigma]
    damp = [1.0 / (1.0 + x) for x in rate]
    speed = jnp.concatenate([wind_speed[...]] * 4, axis=1)
    wind = [speed * x for x in sigma]
    push = [BETA * x for x in sigma]
    towards = jnp.concatenate([wind_dir[...]] * 4, axis=1)
    step = lax.broadcasted_iota(jnp.int32, (pairs, LANES), 0) * 2 + jnp.bitwise_and(
        jnp.right_shift(lax.broadcasted_iota(jnp.int32, (pairs, LANES), 1), 5), 1
    )
    rows[...] = cosine((2.0 * math.pi / ndirs) * step.astype(jnp.float32) - towards)

    def grow(s, carry):
        along = rows[pl.ds(s, 1), :]
        for b in range(lots):
            growth = push[b] * jnp.maximum(wind[b] * along - 1.0, 0.0)
            value = relaid[b, s] * (1.0 + growth) * damp[b]
            quarter = pltpu.roll(value, LANES - 32, 1)
            even = jnp.where(low, value, quarter)
            odd = jnp.where(low, quarter, pltpu.roll(value, 64, 1))
            for i, part in enumerate((even, odd)):
                turned[pl.ds(b * ndirs + 2 * s + i, 8, stride=lots * ndirs), :] = part
        return carry

    low = lane < 32
    lax.fori_loop(0, pairs, grow, 0, unroll=GROW)

    def place(a, carry):
        for b in range(lots):
            spot = pl.ds(pl.multiple_of((a * lots + b) * ndirs, ndirs), ndirs)
            flat = jnp.swapaxes(turned[spot, :], 0, 1)
            for x in range(2):
                out[a * 2 * lots + 2 * b + x] = flat[32 * x : 32 * x + 32]
        spot = pl.ds(a * 2 * lots, 2 * lots)
        pltpu.make_async_copy(out.at[spot], out_at.at[spot], left.at[a]).start()
        return carry

    lax.fori_loop(0, 8, place, 0, unroll=PLACE)
    for a in range(8):
        spot = pl.ds(a * 2 * lots, 2 * lots)
        pltpu.make_async_copy(out.at[spot], out_at.at[spot], left.at[a]).wait()


def local_scoped(ndirs, *refs):
    freqs, dirs, npoints = refs[0].shape
    sums = [
        pltpu.ACC(unit)((3 * npoints // TILE, TILE), jnp.float32)
        for unit in range(2)
        for _ in range(2 * dirs * freqs // 3)
    ]
    pl.run_scoped(lambda *sums: local_kernel(ndirs, *refs, *sums), *sums)


def local_call(
    ndirs, parts, spectrum, neighbours, edge_angle, edge_coef, land_mask, space_order
):
    dirs, freqs, npoints = spectrum.shape
    tiles = npoints // TILE
    near = neighbours.shape[0]
    vmem = pl.BlockSpec(memory_space=pltpu.VMEM)
    return pl.pallas_call(
        functools.partial(local_scoped, ndirs),
        out_shape=jax.ShapeDtypeStruct((parts * dirs * freqs // 4, 2, LANES), jnp.bfloat16),
        in_specs=[pl.BlockSpec(memory_space=pltpu.MemorySpace.HBM)] * 6,
        out_specs=vmem,
        scratch_shapes=[
            pltpu.VMEM((freqs, dirs, npoints), jnp.float32),
            pltpu.VMEM((near, npoints), jnp.int32),
            pltpu.VMEM((near, npoints), jnp.float32),
            pltpu.VMEM((near, npoints), jnp.float32),
            pltpu.VMEM((1, npoints), jnp.int32),
            pltpu.VMEM((1, npoints), jnp.int32),
            pltpu.SemaphoreType.DMA((6,)),
            pltpu.VMEM((dirs, 8, npoints), jnp.float32),
            pltpu.VMEM((TILE // LANES, dirs * freqs * tiles, LANES), jnp.float32),
            pltpu.VMEM((dirs * freqs * tiles, TILE), jnp.bfloat16),
            pltpu.VMEM((TILE // LANES, 2 * dirs * freqs * tiles, LANES), jnp.float32),
            pltpu.VMEM((2 * dirs * freqs * tiles, TILE), jnp.bfloat16),
            pltpu.VMEM((TILE, TILE), jnp.bfloat16),
        ],
        compiler_params=pltpu.CompilerParams(vmem_limit_bytes=40 * 1024 * 1024),
        name="local_step",
    )(
        *(
            pltpu.with_memory_space_constraint(x, pltpu.MemorySpace.HBM)
            for x in (
                spectrum.transpose(1, 0, 2),
                neighbours,
                edge_angle,
                edge_coef,
                land_mask.reshape(1, npoints),
                space_order.reshape(1, npoints),
            )
        )
    )


def finish_call(ndirs, nd, nf, dia_offsets, dia_coef, wind_speed, wind_dir, blocks):
    vmem = pl.BlockSpec(memory_space=pltpu.VMEM)
    smem = pl.BlockSpec(memory_space=pltpu.SMEM)
    lots = blocks.shape[0] // (nd * nf)
    return pl.pallas_call(
        functools.partial(finish_kernel, ndirs),
        out_shape=jax.ShapeDtypeStruct((NFREQ, LANES // 4, ndirs), jnp.float32),
        in_specs=[smem, smem, vmem, vmem, vmem],
        out_specs=pl.BlockSpec(memory_space=pltpu.MemorySpace.HBM),
        scratch_shapes=[
            pltpu.VMEM((2, 2, lots + 2, nd + DSPAN, nf, LANES), jnp.float32),
            pltpu.VMEM((lots, nd, nf, LANES), jnp.float32),
            pltpu.VMEM((nd, LANES), jnp.float32),
            pltpu.VMEM((2 * nf * lots * nd, LANES), jnp.float32),
            pltpu.VMEM((nf * lots * ndirs, LANES), jnp.float32),
            pltpu.VMEM((NFREQ, LANES // 4, ndirs), jnp.float32),
            pltpu.SemaphoreType.DMA((nf,)),
        ],
        compiler_params=pltpu.CompilerParams(vmem_limit_bytes=40 * 1024 * 1024),
        name="finish_step",
    )(dia_offsets, dia_coef, wind_speed, wind_dir, blocks)


def on_device(
    spectrum,
    neighbours,
    edge_angle,
    edge_coef,
    land_mask,
    dia_offsets,
    dia_coef,
    space_order,
    wind_speed,
    wind_dir,
):
    dirs, freqs, npoints = spectrum.shape
    nd, nf = lax.axis_size("dir"), lax.axis_size("freq")
    parts = nd * nf
    blocks = local_call(
        nd * dirs, parts, spectrum, neighbours, edge_angle, edge_coef, land_mask, space_order
    )
    blocks = lax.all_to_all(blocks, ("dir", "freq"), split_axis=0, concat_axis=0, tiled=True)
    npts = npoints // parts
    done = finish_call(
        nd * dirs, nd, nf, dia_offsets, dia_coef,
        wind_speed.reshape(1, npts), wind_dir.reshape(1, npts), blocks,
    )
    return done.transpose(2, 0, 1)


def solution(mesh):
    in_specs = (
        P("dir", "freq", None),
        P(),
        P(),
        P(),
        P(),
        P(),
        P(),
        P(),
        P(("dir", "freq")),
        P(("dir", "freq")),
    )
    out_specs = P(None, None, ("dir", "freq"))
    return jax.shard_map(
        on_device, mesh=mesh, in_specs=in_specs, out_specs=out_specs, check_vma=False
    )
```

```python
import functools
import math

import jax
import jax.numpy as jnp
from jax import lax
from jax.experimental import pallas as pl
from jax.experimental.pallas import tpu as pltpu
from jax.sharding import PartitionSpec as P

NFREQ = 48
DSPAN = 6
FSPAN = 2

SIG_LO = 0.35
SIG_HI = 2.8
DT_NL = 0.1
CDS = 0.05
APM = 0.4
BETA = 0.05
INV_FLOOR = 0.01

LANES = 128
TILE = 256
WIDEN, UNPACK, TRANSFER, GROW, PLACE = 8, 8, 8, 16, 4
STAGE, ADVECT, SWAP = 4, 16, 32
ROUND = 1.5 * 2.0**23
SINE = (1.0, -0.16666667, 0.008333329, -0.00019840701, 2.7518759e-06, -2.3793149e-08)
CENTRE = 0.5


def sigma_of(index):
    return SIG_LO * jnp.exp(index.astype(jnp.float32) * (math.log(SIG_HI / SIG_LO) / (NFREQ - 1)))


def cosine(x):
    turns = (x * (0.5 / math.pi) + ROUND) - ROUND
    h = (x * 0.5 - turns * 3.140625) - turns * (math.pi - 3.140625)
    z = h * h
    p = SINE[-1]
    for c in SINE[-2::-1]:
        p = p * z + c
    s = p * h
    return 1.0 - 2.0 * (s * s)


def one_hot(low, ramp):
    one, none = jnp.ones((), jnp.bfloat16), jnp.zeros((), jnp.bfloat16)
    return jnp.where(ramp == low.astype(jnp.float32).astype(jnp.bfloat16), one, none)


def local_kernel(
    ndirs, spec_at, nbr_at, angle_at, coef_at, mask_at, order_at, out,
    spec, nbr, angle, coef, mask, order, arrived, field, pickf, pick, keepf, keep, ramp, *sums
):
    freqs, dirs, npoints = spec.shape
    tiles = npoints // TILE
    near = nbr.shape[0]
    first_dir = lax.axis_index("dir") * dirs
    first_freq = lax.axis_index("freq") * freqs
    pairs = [(spec_at, spec), (mask_at, mask), (nbr_at, nbr)]
    pairs += [(angle_at, angle), (coef_at, coef), (order_at, order)]
    copies = [
        pltpu.make_async_copy(src, dst, arrived.at[n]) for n, (src, dst) in enumerate(pairs)
    ]
    for copy in copies:
        copy.start()
    sub = lax.broadcasted_iota(jnp.int32, (8, TILE), 0)
    lane = lax.broadcasted_iota(jnp.int32, (8, LANES), 1)
    speed = 0.5 / sigma_of(first_freq + sub)
    ramp[...] = lax.broadcasted_iota(jnp.int32, (TILE, TILE), 0).astype(jnp.float32).astype(jnp.bfloat16)
    pad = jnp.zeros((8 - freqs, TILE), jnp.float32)
    for copy in copies[:2]:
        copy.wait()

    def span(t):
        return pl.ds(pl.multiple_of(t * TILE, TILE), TILE)

    def stage(t, carry):
        at = span(t)
        wet_row = mask[:, at].astype(jnp.float32)
        for i in range(dirs):
            rows = [spec[f, pl.ds(i, 1), at] for f in range(freqs)]
            value = jnp.concatenate(rows + [pad], axis=0)
            field[i, :, at] = value
            shown = value * wet_row - CENTRE
            spot = pl.ds(i * freqs * tiles + t, freqs, stride=tiles)
            for c in range(TILE // LANES):
                pickf[c, spot, :] = shown[:freqs, c * LANES : (c + 1) * LANES]
        return carry

    lax.fori_loop(0, tiles, stage, 0, unroll=STAGE)
    for c in range(TILE // LANES):
        pick[:, c * LANES : (c + 1) * LANES] = pickf[c].astype(jnp.bfloat16)
    for copy in copies[2:5]:
        copy.wait()

    def split(index):
        low = jnp.bitwise_and(index, TILE - 1)
        high = jnp.broadcast_to(jnp.right_shift(index, 8), (8, TILE))
        return one_hot(low, ramp[...]), high

    def issue(job, table, accs, index, chunk):
        unit, slot = job % 2, job // 2 % 2
        hot, high = split(index)
        pltpu.matmul_push_rhs(hot, slot, unit)
        for c, acc in enumerate(accs[unit][slot]):
            rows = table[c * chunk : (c + 1) * chunk, :]
            pltpu.matmul_acc_lhs(acc, rows, load_staged_rhs=slot if c == 0 else None)
        return high

    groups = tiles // 8
    chunk = 3 * tiles
    width = 2 * dirs * freqs
    count = dirs * freqs // 3
    accs = [[sums[(u * 2 + v) * count : (u * 2 + v + 1) * count] for v in range(2)] for u in range(2)]

    def advect(step, carry):
        jobs = [(u, k) for u in range(ADVECT) for k in range(near)]
        highs = {}

        def start(n):
            u, k = jobs[n]
            highs[n] = issue(n, pick, accs, nbr[k : k + 1, span(step * ADVECT + u)], chunk)

        start(0)
        start(1)
        for n, (u, k) in enumerate(jobs):
            t = step * ADVECT + u
            at = span(t)
            if k == 0:
                total = [jnp.zeros((8, TILE), jnp.float32) for _ in range(dirs * freqs)]
                geom = []
                for i in range(dirs):
                    theta = (2.0 * math.pi / ndirs) * (first_dir + i).astype(jnp.float32)
                    bearing = cosine(theta - angle[:, at])
                    geom.append(coef[:, at] * jnp.maximum(bearing, 0.0))
            high = highs.pop(n)
            match = [high == sub + 8 * h for h in range(groups)]
            rows = [geom[i][k : k + 1] for i in range(dirs)]
            unit, slot = n % 2, n // 2 % 2
            for c, acc in enumerate(accs[unit][slot]):
                found = pltpu.matmul_pop(acc)
                for x in range(3):
                    r = c * 3 + x
                    chosen = jnp.zeros((8, TILE), jnp.float32)
                    for h in range(groups):
                        begin = x * tiles + 8 * h
                        chosen = jnp.where(match[h], found[begin : begin + 8], chosen)
                    total[r] = total[r] + rows[r // freqs] * chosen
            if n + 2 < len(jobs):
                start(n + 2)
            if k == near - 1:
                wet_row = mask[:, at].astype(jnp.float32)
                for i in range(dirs):
                    value = field[i, :, at]
                    weight = jnp.sum(geom[i], axis=0, keepdims=True)
                    lines = [
                        jnp.sum(total[i * freqs + f], axis=0, keepdims=True) for f in range(freqs)
                    ]
                    inflow = jnp.concatenate(lines + [pad], axis=0)
                    moved = value + speed * (inflow + weight * (CENTRE - value))
                    old = value.astype(jnp.bfloat16).astype(jnp.float32)
                    for n, part in enumerate((wet_row * old, wet_row * (moved - old))):
                        spot = pl.ds(t * width + i * 2 + n, freqs, stride=2 * dirs)
                        for c in range(TILE // LANES):
                            keepf[c, spot, :] = part[:freqs, c * LANES : (c + 1) * LANES]
        return carry

    lax.fori_loop(0, tiles // ADVECT, advect, 0)
    for c in range(TILE // LANES):
        keep[:, c * LANES : (c + 1) * LANES] = keepf[c].astype(jnp.bfloat16)
    copies[5].wait()

    row = sub[:, :LANES]
    outer = jnp.right_shift(row, 2) == jnp.right_shift(lane, 6)
    inner = jnp.bitwise_and(row, 2) == jnp.bitwise_and(jnp.right_shift(lane, 4), 2)
    first = jnp.bitwise_and(row, 2) == 0

    def swap(step, carry):
        jobs = list(range(SWAP))
        highs = {}
        hots = {}
        accs = [[*sums[: 2 * count]], [*sums[2 * count :]]]

        def push(n):
            hots[n], highs[n] = split(order[:, span(step * SWAP + n)])
            pltpu.matmul_push_rhs(hots[n], n // 2 % 2, n % 2)

        def multiply(n, c):
            rows = keep[c * chunk : (c + 1) * chunk, :]
            slot = n // 2 % 2 if c == 0 else None
            pltpu.matmul_acc_lhs(accs[n % 2][c], rows, load_staged_rhs=slot)

        for n in jobs[:2]:
            push(n)
            for c in range(2 * count):
                multiply(n, c)
        for n in jobs:
            high = highs.pop(n)
            part = [jnp.zeros((8, TILE), jnp.float32) for _ in range(width // 8)]
            if n + 2 < len(jobs):
                push(n + 2)
            for c in range(2 * count):
                found = pltpu.matmul_pop(accs[n % 2][c])
                if n + 2 < len(jobs):
                    multiply(n + 2, c)
                for x in range(chunk // width):
                    match = high == c * (chunk // width) + x
                    for g in range(width // 8):
                        begin = x * width + 8 * g
                        part[g] = jnp.where(match, found[begin : begin + 8], part[g])
            for g, whole in enumerate(part):
                for c in range(TILE // LANES):
                    x = whole[:, c * LANES : (c + 1) * LANES]
                    x = jnp.where(outer, x, pltpu.roll(pltpu.roll(x, 4, 0), 64, 1))
                    after = pltpu.roll(pltpu.roll(x, 6, 0), 32, 1)
                    before = pltpu.roll(pltpu.roll(x, 2, 0), 96, 1)
                    x = jnp.where(inner, x, jnp.where(first, after, before)).astype(jnp.bfloat16)
                    for b in range(4):
                        spot = ((step * SWAP + n) * 8 + c * 4 + b) * (width // 8) + g
                        out[spot] = x[2 * b : 2 * b + 2]
        return carry

    lax.fori_loop(0, tiles // SWAP, swap, 0)


def finish_kernel(
    ndirs, offsets_at, strength_at, speed_at, dir_at, blocks, out_at,
    offsets, strength, wind_speed, wind_dir, arrived, table, relaid, rows, lines, turned, out, left
):
    small = [(offsets_at, offsets), (strength_at, strength)]
    small += [(speed_at, wind_speed), (dir_at, wind_dir)]
    copies = [
        pltpu.make_async_copy(src, dst, arrived.at[n]) for n, (src, dst) in enumerate(small)
    ]
    for copy in copies:
        copy.start()
    pairs = ndirs // 2
    reach = DSPAN // 2
    lots = table.shape[2] - 2
    sub = lax.broadcasted_iota(jnp.int32, (8, LANES), 0)
    lane = lax.broadcasted_iota(jnp.int32, (8, LANES), 1)
    second = jnp.bitwise_and(lane, 32) == 0
    first = lane < 64
    per = 8 * lots

    def turn(x):
        return jnp.where(second, pltpu.roll(x, LANES - 32, 1), pltpu.roll(x, 32, 1))

    def widen(s, carry):
        piece = blocks[pl.ds(s * per, per)].astype(jnp.float32)
        spot = pl.ds(pl.multiple_of(s * 2 * per, 2 * per), 2 * per)
        lines[spot, :] = piece.reshape(2 * per, LANES)
        return carry

    lax.fori_loop(0, pairs, widen, 0, unroll=WIDEN)

    def unpack(s, carry):
        for b in range(lots):
            begin = s * 2 * per + 2 * b
            old = lines[pl.ds(begin, 8, stride=2 * lots), :]
            relaid[b, s] = lines[pl.ds(begin + 1, 8, stride=2 * lots), :]
            other = pltpu.roll(old, 64, 1)
            forms = ((old, turn(old)), (other, turn(other)))
            for i in range(2):
                for j in range(2):
                    table[i, j, b + 1, s + reach] = forms[i][j]
                    if b == 0:
                        shifted = jnp.where(sub == 7, 0.0, pltpu.roll(forms[i][j], 7, 0))
                        table[i, j, lots + 1, s + reach] = shifted
                    if b == lots - 1:
                        shifted = jnp.where(sub == 0, 0.0, pltpu.roll(forms[i][j], 1, 0))
                        table[i, j, 0, s + reach] = shifted
        return carry

    lax.fori_loop(0, pairs, unpack, 0, unroll=UNPACK)
    for i in range(2):
        for j in range(2):
            for b in range(lots + 2):
                for s in range(reach):
                    table[i, j, b, s] = table[i, j, b, s + pairs]
                    table[i, j, b, s + pairs + reach] = table[i, j, b, s + reach]

    for copy in copies:
        copy.wait()
    shapes = []
    for q in range(strength.shape[0]):
        d, m, c = offsets[0, q], offsets[1, q], strength[q]
        at = [jnp.right_shift(m + x, 1) + 1 for x in range(2)]
        to = [jnp.right_shift(d + x, 1) + reach for x in range(2)]
        back_at = [jnp.right_shift(x - m, 1) + 1 for x in range(2)]
        back_to = [jnp.right_shift(x - d, 1) + reach for x in range(2)]
        odd = (jnp.bitwise_and(m, 1), jnp.bitwise_and(d, 1))
        shapes.append((odd, at, to, back_at, back_to, c))

    def transfer(s, carry):
        total = list(carry)
        for b in range(lots):
            body = table[0, 0, b + 1, s + reach]
            plain = jnp.zeros((8, LANES), jnp.float32)
            cross = jnp.zeros((8, LANES), jnp.float32)
            for odd, at, to, back_at, back_to, c in shapes:

                def shifted(at, to):
                    got = [[table[odd[0], odd[1], b + x, s + y] for y in to] for x in at]
                    got = [jnp.where(second, x[0], x[1]) for x in got]
                    return jnp.where(first, got[0], got[1])

                upper, lower = shifted(at, to), shifted(back_at, back_to)
                plain = plain + c * (upper + lower)
                cross = cross + (2.0 * c) * (upper * lower)
            value = body + relaid[b, s] + DT_NL * (body * (body * plain - cross))
            relaid[b, s] = value
            total[b] = total[b] + value
        return tuple(total)

    empty = jnp.zeros((8, LANES), jnp.float32)
    total = lax.fori_loop(0, pairs, transfer, (empty,) * lots, unroll=TRANSFER)

    half = jnp.right_shift(lane, 6)
    sigma = [sigma_of(sub * (2 * lots) + 2 * b + half) for b in range(lots)]
    weight = 1.0 / (ndirs * NFREQ)

    def over_all(terms):
        x = jnp.sum(sum(terms), axis=0, keepdims=True)
        x = jnp.broadcast_to(x, (8, LANES))
        x = x + pltpu.roll(x, 64, 1)
        return x + pltpu.roll(x, 32, 1)

    etot = over_all(total) * weight
    inverse = over_all([x / y for x, y in zip(total, sigma)]) * weight
    msig = jnp.clip(etot / jnp.maximum(inverse, INV_FLOOR), SIG_LO, SIG_HI)
    steep = etot * (msig * msig * msig * msig) / APM
    rate = [CDS * ((x / msig) * (x / msig)) * msig * (steep * steep) for x in sigma]
    damp = [1.0 / (1.0 + x) for x in rate]
    speed = jnp.concatenate([wind_speed[...]] * 4, axis=1)
    wind = [speed * x for x in sigma]
    push = [BETA * x for x in sigma]
    towards = jnp.concatenate([wind_dir[...]] * 4, axis=1)
    step = lax.broadcasted_iota(jnp.int32, (pairs, LANES), 0) * 2 + jnp.bitwise_and(
        jnp.right_shift(lax.broadcasted_iota(jnp.int32, (pairs, LANES), 1), 5), 1
    )
    rows[...] = cosine((2.0 * math.pi / ndirs) * step.astype(jnp.float32) - towards)

    def grow(s, carry):
        along = rows[pl.ds(s, 1), :]
        for b in range(lots):
            growth = push[b] * jnp.maximum(wind[b] * along - 1.0, 0.0)
            value = relaid[b, s] * (1.0 + growth) * damp[b]
            quarter = pltpu.roll(value, LANES - 32, 1)
            even = jnp.where(low, value, quarter)
            odd = jnp.where(low, quarter, pltpu.roll(value, 64, 1))
            for i, part in enumerate((even, odd)):
                turned[pl.ds(b * ndirs + 2 * s + i, 8, stride=lots * ndirs), :] = part
        return carry

    low = lane < 32
    lax.fori_loop(0, pairs, grow, 0, unroll=GROW)

    def place(a, carry):
        for b in range(lots):
            spot = pl.ds(pl.multiple_of((a * lots + b) * ndirs, ndirs), ndirs)
            flat = jnp.swapaxes(turned[spot, :], 0, 1)
            for x in range(2):
                out[a * 2 * lots + 2 * b + x] = flat[32 * x : 32 * x + 32]
        spot = pl.ds(a * 2 * lots, 2 * lots)
        pltpu.make_async_copy(out.at[spot], out_at.at[spot], left.at[a]).start()
        return carry

    lax.fori_loop(0, 8, place, 0, unroll=PLACE)
    for a in range(8):
        spot = pl.ds(a * 2 * lots, 2 * lots)
        pltpu.make_async_copy(out.at[spot], out_at.at[spot], left.at[a]).wait()


def local_scoped(ndirs, *refs):
    freqs, dirs, npoints = refs[0].shape
    sums = [
        pltpu.ACC(unit)((3 * npoints // TILE, TILE), jnp.float32)
        for unit in range(2)
        for _ in range(2 * dirs * freqs // 3)
    ]
    pl.run_scoped(lambda *sums: local_kernel(ndirs, *refs, *sums), *sums)


def local_call(
    ndirs, parts, spectrum, neighbours, edge_angle, edge_coef, land_mask, space_order
):
    dirs, freqs, npoints = spectrum.shape
    tiles = npoints // TILE
    near = neighbours.shape[0]
    vmem = pl.BlockSpec(memory_space=pltpu.VMEM)
    return pl.pallas_call(
        functools.partial(local_scoped, ndirs),
        out_shape=jax.ShapeDtypeStruct((parts * dirs * freqs // 4, 2, LANES), jnp.bfloat16),
        in_specs=[pl.BlockSpec(memory_space=pltpu.MemorySpace.HBM)] * 6,
        out_specs=vmem,
        scratch_shapes=[
            pltpu.VMEM((freqs, dirs, npoints), jnp.float32),
            pltpu.VMEM((near, npoints), jnp.int32),
            pltpu.VMEM((near, npoints), jnp.float32),
            pltpu.VMEM((near, npoints), jnp.float32),
            pltpu.VMEM((1, npoints), jnp.int32),
            pltpu.VMEM((1, npoints), jnp.int32),
            pltpu.SemaphoreType.DMA((6,)),
            pltpu.VMEM((dirs, 8, npoints), jnp.float32),
            pltpu.VMEM((TILE // LANES, dirs * freqs * tiles, LANES), jnp.float32),
            pltpu.VMEM((dirs * freqs * tiles, TILE), jnp.bfloat16),
            pltpu.VMEM((TILE // LANES, 2 * dirs * freqs * tiles, LANES), jnp.float32),
            pltpu.VMEM((2 * dirs * freqs * tiles, TILE), jnp.bfloat16),
            pltpu.VMEM((TILE, TILE), jnp.bfloat16),
        ],
        compiler_params=pltpu.CompilerParams(vmem_limit_bytes=40 * 1024 * 1024),
        name="local_step",
    )(
        *(
            pltpu.with_memory_space_constraint(x, pltpu.MemorySpace.HBM)
            for x in (
                spectrum.transpose(1, 0, 2),
                neighbours,
                edge_angle,
                edge_coef,
                land_mask.reshape(1, npoints),
                space_order.reshape(1, npoints),
            )
        )
    )


def finish_call(ndirs, nd, nf, dia_offsets, dia_coef, wind_speed, wind_dir, blocks):
    vmem = pl.BlockSpec(memory_space=pltpu.VMEM)
    hbm = pl.BlockSpec(memory_space=pltpu.MemorySpace.HBM)
    lots = blocks.shape[0] // (nd * nf)
    return pl.pallas_call(
        functools.partial(finish_kernel, ndirs),
        out_shape=jax.ShapeDtypeStruct((NFREQ, LANES // 4, ndirs), jnp.float32),
        in_specs=[hbm, hbm, hbm, hbm, vmem],
        out_specs=pl.BlockSpec(memory_space=pltpu.MemorySpace.HBM),
        scratch_shapes=[
            pltpu.SMEM(dia_offsets.shape, jnp.int32),
            pltpu.SMEM(dia_coef.shape, jnp.float32),
            pltpu.VMEM(wind_speed.shape, jnp.float32),
            pltpu.VMEM(wind_dir.shape, jnp.float32),
            pltpu.SemaphoreType.DMA((4,)),
            pltpu.VMEM((2, 2, lots + 2, nd + DSPAN, nf, LANES), jnp.float32),
            pltpu.VMEM((lots, nd, nf, LANES), jnp.float32),
            pltpu.VMEM((nd, LANES), jnp.float32),
            pltpu.VMEM((2 * nf * lots * nd, LANES), jnp.float32),
            pltpu.VMEM((nf * lots * ndirs, LANES), jnp.float32),
            pltpu.VMEM((NFREQ, LANES // 4, ndirs), jnp.float32),
            pltpu.SemaphoreType.DMA((nf,)),
        ],
        compiler_params=pltpu.CompilerParams(vmem_limit_bytes=40 * 1024 * 1024),
        name="finish_step",
    )(
        *(
            pltpu.with_memory_space_constraint(x, pltpu.MemorySpace.HBM)
            for x in (dia_offsets, dia_coef, wind_speed, wind_dir)
        ),
        blocks,
    )


def on_device(
    spectrum,
    neighbours,
    edge_angle,
    edge_coef,
    land_mask,
    dia_offsets,
    dia_coef,
    space_order,
    wind_speed,
    wind_dir,
):
    dirs, freqs, npoints = spectrum.shape
    nd, nf = lax.axis_size("dir"), lax.axis_size("freq")
    parts = nd * nf
    blocks = local_call(
        nd * dirs, parts, spectrum, neighbours, edge_angle, edge_coef, land_mask, space_order
    )
    blocks = lax.all_to_all(blocks, ("dir", "freq"), split_axis=0, concat_axis=0, tiled=True)
    npts = npoints // parts
    done = finish_call(
        nd * dirs, nd, nf, dia_offsets, dia_coef,
        wind_speed.reshape(1, npts), wind_dir.reshape(1, npts), blocks,
    )
    return done.transpose(2, 0, 1)


def solution(mesh):
    in_specs = (
        P("dir", "freq", None),
        P(),
        P(),
        P(),
        P(),
        P(),
        P(),
        P(),
        P(("dir", "freq")),
        P(("dir", "freq")),
    )
    out_specs = P(None, None, ("dir", "freq"))
    return jax.shard_map(
        on_device, mesh=mesh, in_specs=in_specs, out_specs=out_specs, check_vma=False
    )
```

```python
import functools
import math

import jax
import jax.numpy as jnp
from jax import lax
from jax.experimental import pallas as pl
from jax.experimental.pallas import tpu as pltpu
from jax.sharding import PartitionSpec as P

NFREQ = 48
DSPAN = 6
FSPAN = 2

SIG_LO = 0.35
SIG_HI = 2.8
DT_NL = 0.1
CDS = 0.05
APM = 0.4
BETA = 0.05
INV_FLOOR = 0.01

LANES = 128
TILE = 256
WIDEN, UNPACK, TRANSFER, GROW, PLACE = 8, 8, 8, 16, 4
STAGE, ADVECT, SWAP = 4, 16, 32
ROUND = 1.5 * 2.0**23
SINE = (1.0, -0.16666667, 0.008333329, -0.00019840701, 2.7518759e-06, -2.3793149e-08)
CENTRE = 0.5


def sigma_of(index):
    return SIG_LO * jnp.exp(index.astype(jnp.float32) * (math.log(SIG_HI / SIG_LO) / (NFREQ - 1)))


def cosine(x):
    turns = (x * (0.5 / math.pi) + ROUND) - ROUND
    h = (x * 0.5 - turns * 3.140625) - turns * (math.pi - 3.140625)
    z = h * h
    p = SINE[-1]
    for c in SINE[-2::-1]:
        p = p * z + c
    s = p * h
    return 1.0 - 2.0 * (s * s)


def one_hot(low, ramp):
    one, none = jnp.ones((), jnp.bfloat16), jnp.zeros((), jnp.bfloat16)
    return jnp.where(ramp == low.astype(jnp.float32).astype(jnp.bfloat16), one, none)


def local_kernel(
    ndirs, spec_at, nbr_at, angle_at, coef_at, mask_at, order_at, out,
    spec, nbr, angle, coef, mask, order, arrived, field, pickf, pick, keepf, keep, ramp, *sums
):
    freqs, dirs, npoints = spec.shape
    tiles = npoints // TILE
    near = nbr.shape[0]
    first_dir = lax.axis_index("dir") * dirs
    first_freq = lax.axis_index("freq") * freqs
    pairs = [(spec_at, spec), (mask_at, mask), (nbr_at, nbr)]
    pairs += [(angle_at, angle), (coef_at, coef), (order_at, order)]
    copies = [
        pltpu.make_async_copy(src, dst, arrived.at[n]) for n, (src, dst) in enumerate(pairs)
    ]
    for copy in copies:
        copy.start()
    sub = lax.broadcasted_iota(jnp.int32, (8, TILE), 0)
    lane = lax.broadcasted_iota(jnp.int32, (8, LANES), 1)
    speed = 0.5 / sigma_of(first_freq + sub)
    ramp[...] = lax.broadcasted_iota(jnp.int32, (TILE, TILE), 0).astype(jnp.float32).astype(jnp.bfloat16)
    pad = jnp.zeros((8 - freqs, TILE), jnp.float32)
    for copy in copies[:2]:
        copy.wait()

    def span(t):
        return pl.ds(pl.multiple_of(t * TILE, TILE), TILE)

    def stage(t, carry):
        at = span(t)
        wet_row = mask[:, at].astype(jnp.float32)
        for i in range(dirs):
            rows = [spec[f, pl.ds(i, 1), at] for f in range(freqs)]
            value = jnp.concatenate(rows + [pad], axis=0)
            field[i, :, at] = value
            shown = value * wet_row - CENTRE
            spot = pl.ds(i * freqs * tiles + t, freqs, stride=tiles)
            for c in range(TILE // LANES):
                pickf[c, spot, :] = shown[:freqs, c * LANES : (c + 1) * LANES]
        return carry

    lax.fori_loop(0, tiles, stage, 0, unroll=STAGE)
    for c in range(TILE // LANES):
        pick[:, c * LANES : (c + 1) * LANES] = pickf[c, : pick.shape[0]].astype(jnp.bfloat16)
    for copy in copies[2:5]:
        copy.wait()

    def split(index):
        low = jnp.bitwise_and(index, TILE - 1)
        high = jnp.broadcast_to(jnp.right_shift(index, 8), (8, TILE))
        return one_hot(low, ramp[...]), high

    def issue(job, table, accs, index, chunk):
        unit, slot = job % 2, job // 2 % 2
        hot, high = split(index)
        pltpu.matmul_push_rhs(hot, slot, unit)
        for c, acc in enumerate(accs[unit][slot]):
            rows = table[c * chunk : (c + 1) * chunk, :]
            pltpu.matmul_acc_lhs(acc, rows, load_staged_rhs=slot if c == 0 else None)
        return high

    groups = tiles // 8
    chunk = 3 * tiles
    width = 2 * dirs * freqs
    count = dirs * freqs // 3
    accs = [[sums[(u * 2 + v) * count : (u * 2 + v + 1) * count] for v in range(2)] for u in range(2)]

    def advect(step, carry):
        jobs = [(u, k) for u in range(ADVECT) for k in range(near)]
        highs = {}

        def start(n):
            u, k = jobs[n]
            highs[n] = issue(n, pick, accs, nbr[k : k + 1, span(step * ADVECT + u)], chunk)

        start(0)
        start(1)
        for n, (u, k) in enumerate(jobs):
            t = step * ADVECT + u
            at = span(t)
            if k == 0:
                total = [jnp.zeros((8, TILE), jnp.float32) for _ in range(dirs * freqs)]
                geom = []
                for i in range(dirs):
                    theta = (2.0 * math.pi / ndirs) * (first_dir + i).astype(jnp.float32)
                    bearing = cosine(theta - angle[:, at])
                    geom.append(coef[:, at] * jnp.maximum(bearing, 0.0))
            high = highs.pop(n)
            match = [high == sub + 8 * h for h in range(groups)]
            rows = [geom[i][k : k + 1] for i in range(dirs)]
            unit, slot = n % 2, n // 2 % 2
            for c, acc in enumerate(accs[unit][slot]):
                found = pltpu.matmul_pop(acc)
                for x in range(3):
                    r = c * 3 + x
                    chosen = jnp.zeros((8, TILE), jnp.float32)
                    for h in range(groups):
                        begin = x * tiles + 8 * h
                        chosen = jnp.where(match[h], found[begin : begin + 8], chosen)
                    total[r] = total[r] + rows[r // freqs] * chosen
            if n + 2 < len(jobs):
                start(n + 2)
            if k == near - 1:
                wet_row = mask[:, at].astype(jnp.float32)
                for i in range(dirs):
                    value = field[i, :, at]
                    weight = jnp.sum(geom[i], axis=0, keepdims=True)
                    lines = [
                        jnp.sum(total[i * freqs + f], axis=0, keepdims=True) for f in range(freqs)
                    ]
                    inflow = jnp.concatenate(lines + [pad], axis=0)
                    moved = value + speed * (inflow + weight * (CENTRE - value))
                    old = value.astype(jnp.bfloat16).astype(jnp.float32)
                    for n, part in enumerate((wet_row * old, wet_row * (moved - old))):
                        spot = pl.ds(t * width + i * 2 + n, freqs, stride=2 * dirs)
                        for c in range(TILE // LANES):
                            keepf[c, spot, :] = part[:freqs, c * LANES : (c + 1) * LANES]
        return carry

    lax.fori_loop(0, tiles // ADVECT, advect, 0)
    for c in range(TILE // LANES):
        keep[:, c * LANES : (c + 1) * LANES] = keepf[c, : keep.shape[0]].astype(jnp.bfloat16)
    copies[5].wait()

    row = sub[:, :LANES]
    outer = jnp.right_shift(row, 2) == jnp.right_shift(lane, 6)
    inner = jnp.bitwise_and(row, 2) == jnp.bitwise_and(jnp.right_shift(lane, 4), 2)
    first = jnp.bitwise_and(row, 2) == 0

    def swap(step, carry):
        jobs = list(range(SWAP))
        highs = {}
        hots = {}
        accs = [[*sums[: 2 * count]], [*sums[2 * count :]]]

        def push(n):
            hots[n], highs[n] = split(order[:, span(step * SWAP + n)])
            pltpu.matmul_push_rhs(hots[n], n // 2 % 2, n % 2)

        def multiply(n, c):
            rows = keep[c * chunk : (c + 1) * chunk, :]
            slot = n // 2 % 2 if c == 0 else None
            pltpu.matmul_acc_lhs(accs[n % 2][c], rows, load_staged_rhs=slot)

        for n in jobs[:2]:
            push(n)
            for c in range(2 * count):
                multiply(n, c)
        for n in jobs:
            high = highs.pop(n)
            part = [jnp.zeros((8, TILE), jnp.float32) for _ in range(width // 8)]
            if n + 2 < len(jobs):
                push(n + 2)
            for c in range(2 * count):
                found = pltpu.matmul_pop(accs[n % 2][c])
                if n + 2 < len(jobs):
                    multiply(n + 2, c)
                for x in range(chunk // width):
                    match = high == c * (chunk // width) + x
                    for g in range(width // 8):
                        begin = x * width + 8 * g
                        part[g] = jnp.where(match, found[begin : begin + 8], part[g])
            for g, whole in enumerate(part):
                for c in range(TILE // LANES):
                    x = whole[:, c * LANES : (c + 1) * LANES]
                    x = jnp.where(outer, x, pltpu.roll(pltpu.roll(x, 4, 0), 64, 1))
                    after = pltpu.roll(pltpu.roll(x, 6, 0), 32, 1)
                    before = pltpu.roll(pltpu.roll(x, 2, 0), 96, 1)
                    x = jnp.where(inner, x, jnp.where(first, after, before)).astype(jnp.bfloat16)
                    for b in range(4):
                        spot = ((step * SWAP + n) * 8 + c * 4 + b) * (width // 8) + g
                        out[spot] = x[2 * b : 2 * b + 2]
        return carry

    lax.fori_loop(0, tiles // SWAP, swap, 0)


def finish_kernel(
    ndirs, offsets_at, strength_at, speed_at, dir_at, blocks, out_at,
    offsets, strength, wind_speed, wind_dir, arrived, table, relaid, rows, lines, turned, out, left
):
    small = [(offsets_at, offsets), (strength_at, strength)]
    small += [(speed_at, wind_speed), (dir_at, wind_dir)]
    copies = [
        pltpu.make_async_copy(src, dst, arrived.at[n]) for n, (src, dst) in enumerate(small)
    ]
    for copy in copies:
        copy.start()
    pairs = ndirs // 2
    reach = DSPAN // 2
    lots = table.shape[2] - 2
    sub = lax.broadcasted_iota(jnp.int32, (8, LANES), 0)
    lane = lax.broadcasted_iota(jnp.int32, (8, LANES), 1)
    second = jnp.bitwise_and(lane, 32) == 0
    first = lane < 64
    per = 8 * lots

    def turn(x):
        return jnp.where(second, pltpu.roll(x, LANES - 32, 1), pltpu.roll(x, 32, 1))

    def widen(s, carry):
        piece = blocks[pl.ds(s * per, per)].astype(jnp.float32)
        spot = pl.ds(pl.multiple_of(s * 2 * per, 2 * per), 2 * per)
        lines[spot, :] = piece.reshape(2 * per, LANES)
        return carry

    lax.fori_loop(0, pairs, widen, 0, unroll=WIDEN)

    def unpack(s, carry):
        for b in range(lots):
            begin = s * 2 * per + 2 * b
            old = lines[pl.ds(begin, 8, stride=2 * lots), :]
            relaid[b, s] = lines[pl.ds(begin + 1, 8, stride=2 * lots), :]
            other = pltpu.roll(old, 64, 1)
            forms = ((old, turn(old)), (other, turn(other)))
            for i in range(2):
                for j in range(2):
                    table[i, j, b + 1, s + reach] = forms[i][j]
                    if b == 0:
                        shifted = jnp.where(sub == 7, 0.0, pltpu.roll(forms[i][j], 7, 0))
                        table[i, j, lots + 1, s + reach] = shifted
                    if b == lots - 1:
                        shifted = jnp.where(sub == 0, 0.0, pltpu.roll(forms[i][j], 1, 0))
                        table[i, j, 0, s + reach] = shifted
        return carry

    lax.fori_loop(0, pairs, unpack, 0, unroll=UNPACK)
    for i in range(2):
        for j in range(2):
            for b in range(lots + 2):
                for s in range(reach):
                    table[i, j, b, s] = table[i, j, b, s + pairs]
                    table[i, j, b, s + pairs + reach] = table[i, j, b, s + reach]

    for copy in copies:
        copy.wait()
    shapes = []
    for q in range(strength.shape[0]):
        d, m, c = offsets[0, q], offsets[1, q], strength[q]
        at = [jnp.right_shift(m + x, 1) + 1 for x in range(2)]
        to = [jnp.right_shift(d + x, 1) + reach for x in range(2)]
        back_at = [jnp.right_shift(x - m, 1) + 1 for x in range(2)]
        back_to = [jnp.right_shift(x - d, 1) + reach for x in range(2)]
        odd = (jnp.bitwise_and(m, 1), jnp.bitwise_and(d, 1))
        shapes.append((odd, at, to, back_at, back_to, c))

    def transfer(s, carry):
        total = list(carry)
        for b in range(lots):
            body = table[0, 0, b + 1, s + reach]
            plain = jnp.zeros((8, LANES), jnp.float32)
            cross = jnp.zeros((8, LANES), jnp.float32)
            for odd, at, to, back_at, back_to, c in shapes:

                def shifted(at, to):
                    got = [[table[odd[0], odd[1], b + x, s + y] for y in to] for x in at]
                    got = [jnp.where(second, x[0], x[1]) for x in got]
                    return jnp.where(first, got[0], got[1])

                upper, lower = shifted(at, to), shifted(back_at, back_to)
                plain = plain + c * (upper + lower)
                cross = cross + (2.0 * c) * (upper * lower)
            value = body + relaid[b, s] + DT_NL * (body * (body * plain - cross))
            relaid[b, s] = value
            total[b] = total[b] + value
        return tuple(total)

    empty = jnp.zeros((8, LANES), jnp.float32)
    total = lax.fori_loop(0, pairs, transfer, (empty,) * lots, unroll=TRANSFER)

    half = jnp.right_shift(lane, 6)
    sigma = [sigma_of(sub * (2 * lots) + 2 * b + half) for b in range(lots)]
    weight = 1.0 / (ndirs * NFREQ)

    def over_all(terms):
        x = jnp.sum(sum(terms), axis=0, keepdims=True)
        x = jnp.broadcast_to(x, (8, LANES))
        x = x + pltpu.roll(x, 64, 1)
        return x + pltpu.roll(x, 32, 1)

    etot = over_all(total) * weight
    inverse = over_all([x / y for x, y in zip(total, sigma)]) * weight
    msig = jnp.clip(etot / jnp.maximum(inverse, INV_FLOOR), SIG_LO, SIG_HI)
    steep = etot * (msig * msig * msig * msig) / APM
    rate = [CDS * ((x / msig) * (x / msig)) * msig * (steep * steep) for x in sigma]
    damp = [1.0 / (1.0 + x) for x in rate]
    speed = jnp.concatenate([wind_speed[...]] * 4, axis=1)
    wind = [speed * x for x in sigma]
    push = [BETA * x for x in sigma]
    towards = jnp.concatenate([wind_dir[...]] * 4, axis=1)
    step = lax.broadcasted_iota(jnp.int32, (pairs, LANES), 0) * 2 + jnp.bitwise_and(
        jnp.right_shift(lax.broadcasted_iota(jnp.int32, (pairs, LANES), 1), 5), 1
    )
    rows[...] = cosine((2.0 * math.pi / ndirs) * step.astype(jnp.float32) - towards)

    def grow(s, carry):
        along = rows[pl.ds(s, 1), :]
        for b in range(lots):
            growth = push[b] * jnp.maximum(wind[b] * along - 1.0, 0.0)
            value = relaid[b, s] * (1.0 + growth) * damp[b]
            quarter = pltpu.roll(value, LANES - 32, 1)
            even = jnp.where(low, value, quarter)
            odd = jnp.where(low, quarter, pltpu.roll(value, 64, 1))
            for i, part in enumerate((even, odd)):
                turned[pl.ds(b * ndirs + 2 * s + i, 8, stride=lots * ndirs), :] = part
        return carry

    low = lane < 32
    lax.fori_loop(0, pairs, grow, 0, unroll=GROW)

    def place(a, carry):
        for b in range(lots):
            spot = pl.ds(pl.multiple_of((a * lots + b) * ndirs, ndirs), ndirs)
            flat = jnp.swapaxes(turned[spot, :], 0, 1)
            for x in range(2):
                out[a * 2 * lots + 2 * b + x] = flat[32 * x : 32 * x + 32]
        spot = pl.ds(a * 2 * lots, 2 * lots)
        pltpu.make_async_copy(out.at[spot], out_at.at[spot], left.at[a]).start()
        return carry

    lax.fori_loop(0, 8, place, 0, unroll=PLACE)
    for a in range(8):
        spot = pl.ds(a * 2 * lots, 2 * lots)
        pltpu.make_async_copy(out.at[spot], out_at.at[spot], left.at[a]).wait()


def local_scoped(ndirs, *refs):
    freqs, dirs, npoints = refs[0].shape
    sums = [
        pltpu.ACC(unit)((3 * npoints // TILE, TILE), jnp.float32)
        for unit in range(2)
        for _ in range(2 * dirs * freqs // 3)
    ]
    pl.run_scoped(lambda *sums: local_kernel(ndirs, *refs, *sums), *sums)


def local_call(
    ndirs, parts, spectrum, neighbours, edge_angle, edge_coef, land_mask, space_order
):
    dirs, freqs, npoints = spectrum.shape
    tiles = npoints // TILE
    near = neighbours.shape[0]
    vmem = pl.BlockSpec(memory_space=pltpu.VMEM)
    return pl.pallas_call(
        functools.partial(local_scoped, ndirs),
        out_shape=jax.ShapeDtypeStruct((parts * dirs * freqs // 4, 2, LANES), jnp.bfloat16),
        in_specs=[pl.BlockSpec(memory_space=pltpu.MemorySpace.HBM)] * 6,
        out_specs=vmem,
        scratch_shapes=[
            pltpu.VMEM((freqs, dirs, npoints), jnp.float32),
            pltpu.VMEM((near, npoints), jnp.int32),
            pltpu.VMEM((near, npoints), jnp.float32),
            pltpu.VMEM((near, npoints), jnp.float32),
            pltpu.VMEM((1, npoints), jnp.int32),
            pltpu.VMEM((1, npoints), jnp.int32),
            pltpu.SemaphoreType.DMA((6,)),
            pltpu.VMEM((dirs, 8, npoints), jnp.float32),
            pltpu.VMEM((TILE // LANES, (dirs * freqs + 2) * tiles, LANES), jnp.float32),
            pltpu.VMEM((dirs * freqs * tiles, TILE), jnp.bfloat16),
            pltpu.VMEM((TILE // LANES, 2 * dirs * freqs * tiles + 8, LANES), jnp.float32),
            pltpu.VMEM((2 * dirs * freqs * tiles, TILE), jnp.bfloat16),
            pltpu.VMEM((TILE, TILE), jnp.bfloat16),
        ],
        compiler_params=pltpu.CompilerParams(vmem_limit_bytes=40 * 1024 * 1024),
        name="local_step",
    )(
        *(
            pltpu.with_memory_space_constraint(x, pltpu.MemorySpace.HBM)
            for x in (
                spectrum.transpose(1, 0, 2),
                neighbours,
                edge_angle,
                edge_coef,
                land_mask.reshape(1, npoints),
                space_order.reshape(1, npoints),
            )
        )
    )


def finish_call(ndirs, nd, nf, dia_offsets, dia_coef, wind_speed, wind_dir, blocks):
    vmem = pl.BlockSpec(memory_space=pltpu.VMEM)
    hbm = pl.BlockSpec(memory_space=pltpu.MemorySpace.HBM)
    lots = blocks.shape[0] // (nd * nf)
    return pl.pallas_call(
        functools.partial(finish_kernel, ndirs),
        out_shape=jax.ShapeDtypeStruct((NFREQ, LANES // 4, ndirs), jnp.float32),
        in_specs=[hbm, hbm, hbm, hbm, vmem],
        out_specs=pl.BlockSpec(memory_space=pltpu.MemorySpace.HBM),
        scratch_shapes=[
            pltpu.SMEM(dia_offsets.shape, jnp.int32),
            pltpu.SMEM(dia_coef.shape, jnp.float32),
            pltpu.VMEM(wind_speed.shape, jnp.float32),
            pltpu.VMEM(wind_dir.shape, jnp.float32),
            pltpu.SemaphoreType.DMA((4,)),
            pltpu.VMEM((2, 2, lots + 2, nd + DSPAN, nf, LANES), jnp.float32),
            pltpu.VMEM((lots, nd, nf, LANES), jnp.float32),
            pltpu.VMEM((nd, LANES), jnp.float32),
            pltpu.VMEM((2 * nf * lots * nd, LANES), jnp.float32),
            pltpu.VMEM((nf * lots * ndirs, LANES), jnp.float32),
            pltpu.VMEM((NFREQ, LANES // 4, ndirs), jnp.float32),
            pltpu.SemaphoreType.DMA((nf,)),
        ],
        compiler_params=pltpu.CompilerParams(vmem_limit_bytes=40 * 1024 * 1024),
        name="finish_step",
    )(
        *(
            pltpu.with_memory_space_constraint(x, pltpu.MemorySpace.HBM)
            for x in (dia_offsets, dia_coef, wind_speed, wind_dir)
        ),
        blocks,
    )


def on_device(
    spectrum,
    neighbours,
    edge_angle,
    edge_coef,
    land_mask,
    dia_offsets,
    dia_coef,
    space_order,
    wind_speed,
    wind_dir,
):
    dirs, freqs, npoints = spectrum.shape
    nd, nf = lax.axis_size("dir"), lax.axis_size("freq")
    parts = nd * nf
    blocks = local_call(
        nd * dirs, parts, spectrum, neighbours, edge_angle, edge_coef, land_mask, space_order
    )
    blocks = lax.all_to_all(blocks, ("dir", "freq"), split_axis=0, concat_axis=0, tiled=True)
    npts = npoints // parts
    done = finish_call(
        nd * dirs, nd, nf, dia_offsets, dia_coef,
        wind_speed.reshape(1, npts), wind_dir.reshape(1, npts), blocks,
    )
    return done.transpose(2, 0, 1)


def solution(mesh):
    in_specs = (
        P("dir", "freq", None),
        P(),
        P(),
        P(),
        P(),
        P(),
        P(),
        P(),
        P(("dir", "freq")),
        P(("dir", "freq")),
    )
    out_specs = P(None, None, ("dir", "freq"))
    return jax.shard_map(
        on_device, mesh=mesh, in_specs=in_specs, out_specs=out_specs, check_vma=False
    )
```

```python
import functools
import math

import jax
import jax.numpy as jnp
from jax import lax
from jax.experimental import pallas as pl
from jax.experimental.pallas import tpu as pltpu
from jax.sharding import PartitionSpec as P

NFREQ = 48
DSPAN = 6
FSPAN = 2

SIG_LO = 0.35
SIG_HI = 2.8
DT_NL = 0.1
CDS = 0.05
APM = 0.4
BETA = 0.05
INV_FLOOR = 0.01

LANES = 128
TILE = 256
WIDEN, UNPACK, TRANSFER, GROW, PLACE = 8, 8, 16, 16, 8
STAGE, ADVECT, SWAP = 4, 32, 32
ROUND = 1.5 * 2.0**23
SINE = (1.0, -0.16666667, 0.008333329, -0.00019840701, 2.7518759e-06, -2.3793149e-08)
CENTRE = 0.5


def sigma_of(index):
    return SIG_LO * jnp.exp(index.astype(jnp.float32) * (math.log(SIG_HI / SIG_LO) / (NFREQ - 1)))


def cosine(x):
    turns = (x * (0.5 / math.pi) + ROUND) - ROUND
    h = (x * 0.5 - turns * 3.140625) - turns * (math.pi - 3.140625)
    z = h * h
    p = SINE[-1]
    for c in SINE[-2::-1]:
        p = p * z + c
    s = p * h
    return 1.0 - 2.0 * (s * s)


def one_hot(low, ramp):
    one, none = jnp.ones((), jnp.bfloat16), jnp.zeros((), jnp.bfloat16)
    return jnp.where(ramp == low.astype(jnp.float32).astype(jnp.bfloat16), one, none)


def local_kernel(
    ndirs, spec_at, nbr_at, angle_at, coef_at, mask_at, order_at, out,
    spec, nbr, angle, coef, mask, order, arrived, field, pickf, pick, keepf, keep, ramp, *sums
):
    freqs, dirs, npoints = spec.shape
    tiles = npoints // TILE
    near = nbr.shape[0]
    first_dir = lax.axis_index("dir") * dirs
    first_freq = lax.axis_index("freq") * freqs
    pairs = [(spec_at, spec), (mask_at, mask), (nbr_at, nbr)]
    pairs += [(angle_at, angle), (coef_at, coef), (order_at, order)]
    copies = [
        pltpu.make_async_copy(src, dst, arrived.at[n]) for n, (src, dst) in enumerate(pairs)
    ]
    for copy in copies:
        copy.start()
    sub = lax.broadcasted_iota(jnp.int32, (8, TILE), 0)
    lane = lax.broadcasted_iota(jnp.int32, (8, LANES), 1)
    speed = 0.5 / sigma_of(first_freq + sub)
    ramp[...] = lax.broadcasted_iota(jnp.int32, (TILE, TILE), 0).astype(jnp.float32).astype(jnp.bfloat16)
    pad = jnp.zeros((8 - freqs, TILE), jnp.float32)
    for copy in copies[:2]:
        copy.wait()

    def span(t):
        return pl.ds(pl.multiple_of(t * TILE, TILE), TILE)

    def stage(t, carry):
        at = span(t)
        wet_row = mask[:, at].astype(jnp.float32)
        for i in range(dirs):
            rows = [spec[f, pl.ds(i, 1), at] for f in range(freqs)]
            value = jnp.concatenate(rows + [pad], axis=0)
            field[i, :, at] = value
            shown = value * wet_row - CENTRE
            spot = pl.ds(i * freqs * tiles + t, freqs, stride=tiles)
            for c in range(TILE // LANES):
                pickf[c, spot, :] = shown[:freqs, c * LANES : (c + 1) * LANES]
        return carry

    lax.fori_loop(0, tiles, stage, 0, unroll=STAGE)
    for c in range(TILE // LANES):
        pick[:, c * LANES : (c + 1) * LANES] = pickf[c, : pick.shape[0]].astype(jnp.bfloat16)
    for copy in copies[2:5]:
        copy.wait()

    def split(index):
        low = jnp.bitwise_and(index, TILE - 1)
        high = jnp.broadcast_to(jnp.right_shift(index, 8), (8, TILE))
        return one_hot(low, ramp[...]), high

    def issue(job, table, accs, index, chunk):
        unit, slot = job % 2, job // 2 % 2
        hot, high = split(index)
        pltpu.matmul_push_rhs(hot, slot, unit)
        for c, acc in enumerate(accs[unit][slot]):
            rows = table[c * chunk : (c + 1) * chunk, :]
            pltpu.matmul_acc_lhs(acc, rows, load_staged_rhs=slot if c == 0 else None)
        return high

    groups = tiles // 8
    chunk = 3 * tiles
    width = 2 * dirs * freqs
    count = dirs * freqs // 3
    accs = [[sums[(u * 2 + v) * count : (u * 2 + v + 1) * count] for v in range(2)] for u in range(2)]

    def advect(step, carry):
        jobs = [(u, k) for u in range(ADVECT) for k in range(near)]
        highs = {}

        def start(n):
            u, k = jobs[n]
            highs[n] = issue(n, pick, accs, nbr[k : k + 1, span(step * ADVECT + u)], chunk)

        start(0)
        start(1)
        for n, (u, k) in enumerate(jobs):
            t = step * ADVECT + u
            at = span(t)
            if k == 0:
                total = [jnp.zeros((8, TILE), jnp.float32) for _ in range(dirs * freqs)]
                geom = []
                for i in range(dirs):
                    theta = (2.0 * math.pi / ndirs) * (first_dir + i).astype(jnp.float32)
                    bearing = cosine(theta - angle[:, at])
                    geom.append(coef[:, at] * jnp.maximum(bearing, 0.0))
            high = highs.pop(n)
            match = [high == sub + 8 * h for h in range(groups)]
            rows = [geom[i][k : k + 1] for i in range(dirs)]
            unit, slot = n % 2, n // 2 % 2
            for c, acc in enumerate(accs[unit][slot]):
                found = pltpu.matmul_pop(acc)
                for x in range(3):
                    r = c * 3 + x
                    chosen = jnp.zeros((8, TILE), jnp.float32)
                    for h in range(groups):
                        begin = x * tiles + 8 * h
                        chosen = jnp.where(match[h], found[begin : begin + 8], chosen)
                    total[r] = total[r] + rows[r // freqs] * chosen
            if n + 2 < len(jobs):
                start(n + 2)
            if k == near - 1:
                wet_row = mask[:, at].astype(jnp.float32)
                for i in range(dirs):
                    value = field[i, :, at]
                    weight = jnp.sum(geom[i], axis=0, keepdims=True)
                    lines = [
                        jnp.sum(total[i * freqs + f], axis=0, keepdims=True) for f in range(freqs)
                    ]
                    inflow = jnp.concatenate(lines + [pad], axis=0)
                    moved = value + speed * (inflow + weight * (CENTRE - value))
                    old = value.astype(jnp.bfloat16).astype(jnp.float32)
                    for n, part in enumerate((wet_row * old, wet_row * (moved - old))):
                        spot = pl.ds(t * width + i * 2 + n, freqs, stride=2 * dirs)
                        for c in range(TILE // LANES):
                            keepf[c, spot, :] = part[:freqs, c * LANES : (c + 1) * LANES]
        return carry

    lax.fori_loop(0, tiles // ADVECT, advect, 0)
    for c in range(TILE // LANES):
        keep[:, c * LANES : (c + 1) * LANES] = keepf[c, : keep.shape[0]].astype(jnp.bfloat16)
    copies[5].wait()

    row = sub[:, :LANES]
    outer = jnp.right_shift(row, 2) == jnp.right_shift(lane, 6)
    inner = jnp.bitwise_and(row, 2) == jnp.bitwise_and(jnp.right_shift(lane, 4), 2)
    first = jnp.bitwise_and(row, 2) == 0

    def swap(step, carry):
        jobs = list(range(SWAP))
        highs = {}
        hots = {}
        accs = [[*sums[: 2 * count]], [*sums[2 * count :]]]

        def push(n):
            hots[n], highs[n] = split(order[:, span(step * SWAP + n)])
            pltpu.matmul_push_rhs(hots[n], n // 2 % 2, n % 2)

        def multiply(n, c):
            rows = keep[c * chunk : (c + 1) * chunk, :]
            slot = n // 2 % 2 if c == 0 else None
            pltpu.matmul_acc_lhs(accs[n % 2][c], rows, load_staged_rhs=slot)

        for n in jobs[:2]:
            push(n)
            for c in range(2 * count):
                multiply(n, c)
        for n in jobs:
            high = highs.pop(n)
            part = [jnp.zeros((8, TILE), jnp.float32) for _ in range(width // 8)]
            if n + 2 < len(jobs):
                push(n + 2)
            for c in range(2 * count):
                found = pltpu.matmul_pop(accs[n % 2][c])
                if n + 2 < len(jobs):
                    multiply(n + 2, c)
                for x in range(chunk // width):
                    match = high == c * (chunk // width) + x
                    for g in range(width // 8):
                        begin = x * width + 8 * g
                        part[g] = jnp.where(match, found[begin : begin + 8], part[g])
            for g, whole in enumerate(part):
                for c in range(TILE // LANES):
                    x = whole[:, c * LANES : (c + 1) * LANES]
                    x = jnp.where(outer, x, pltpu.roll(pltpu.roll(x, 4, 0), 64, 1))
                    after = pltpu.roll(pltpu.roll(x, 6, 0), 32, 1)
                    before = pltpu.roll(pltpu.roll(x, 2, 0), 96, 1)
                    x = jnp.where(inner, x, jnp.where(first, after, before)).astype(jnp.bfloat16)
                    for b in range(4):
                        spot = ((step * SWAP + n) * 8 + c * 4 + b) * (width // 8) + g
                        out[spot] = x[2 * b : 2 * b + 2]
        return carry

    lax.fori_loop(0, tiles // SWAP, swap, 0)


def finish_kernel(
    ndirs, offsets_at, strength_at, speed_at, dir_at, blocks, out_at,
    offsets, strength, wind_speed, wind_dir, arrived, table, relaid, rows, lines, turned, out, left
):
    small = [(offsets_at, offsets), (strength_at, strength)]
    small += [(speed_at, wind_speed), (dir_at, wind_dir)]
    copies = [
        pltpu.make_async_copy(src, dst, arrived.at[n]) for n, (src, dst) in enumerate(small)
    ]
    for copy in copies:
        copy.start()
    pairs = ndirs // 2
    reach = DSPAN // 2
    lots = table.shape[2] - 2
    sub = lax.broadcasted_iota(jnp.int32, (8, LANES), 0)
    lane = lax.broadcasted_iota(jnp.int32, (8, LANES), 1)
    second = jnp.bitwise_and(lane, 32) == 0
    first = lane < 64
    per = 8 * lots

    def turn(x):
        return jnp.where(second, pltpu.roll(x, LANES - 32, 1), pltpu.roll(x, 32, 1))

    def widen(s, carry):
        piece = blocks[pl.ds(s * per, per)].astype(jnp.float32)
        spot = pl.ds(pl.multiple_of(s * 2 * per, 2 * per), 2 * per)
        lines[spot, :] = piece.reshape(2 * per, LANES)
        return carry

    lax.fori_loop(0, pairs, widen, 0, unroll=WIDEN)

    def unpack(s, carry):
        for b in range(lots):
            begin = s * 2 * per + 2 * b
            old = lines[pl.ds(begin, 8, stride=2 * lots), :]
            relaid[b, s] = lines[pl.ds(begin + 1, 8, stride=2 * lots), :]
            other = pltpu.roll(old, 64, 1)
            forms = ((old, turn(old)), (other, turn(other)))
            for i in range(2):
                for j in range(2):
                    table[i, j, b + 1, s + reach] = forms[i][j]
                    if b == 0:
                        shifted = jnp.where(sub == 7, 0.0, pltpu.roll(forms[i][j], 7, 0))
                        table[i, j, lots + 1, s + reach] = shifted
                    if b == lots - 1:
                        shifted = jnp.where(sub == 0, 0.0, pltpu.roll(forms[i][j], 1, 0))
                        table[i, j, 0, s + reach] = shifted
        return carry

    lax.fori_loop(0, pairs, unpack, 0, unroll=UNPACK)
    for i in range(2):
        for j in range(2):
            for b in range(lots + 2):
                for s in range(reach):
                    table[i, j, b, s] = table[i, j, b, s + pairs]
                    table[i, j, b, s + pairs + reach] = table[i, j, b, s + reach]

    for copy in copies:
        copy.wait()
    shapes = []
    for q in range(strength.shape[0]):
        d, m, c = offsets[0, q], offsets[1, q], strength[q]
        at = [jnp.right_shift(m + x, 1) + 1 for x in range(2)]
        to = [jnp.right_shift(d + x, 1) + reach for x in range(2)]
        back_at = [jnp.right_shift(x - m, 1) + 1 for x in range(2)]
        back_to = [jnp.right_shift(x - d, 1) + reach for x in range(2)]
        odd = (jnp.bitwise_and(m, 1), jnp.bitwise_and(d, 1))
        shapes.append((odd, at, to, back_at, back_to, c))

    def transfer(s, carry):
        total = list(carry)
        for b in range(lots):
            body = table[0, 0, b + 1, s + reach]
            plain = jnp.zeros((8, LANES), jnp.float32)
            cross = jnp.zeros((8, LANES), jnp.float32)
            for odd, at, to, back_at, back_to, c in shapes:

                def shifted(at, to):
                    got = [[table[odd[0], odd[1], b + x, s + y] for y in to] for x in at]
                    got = [jnp.where(second, x[0], x[1]) for x in got]
                    return jnp.where(first, got[0], got[1])

                upper, lower = shifted(at, to), shifted(back_at, back_to)
                plain = plain + c * (upper + lower)
                cross = cross + (2.0 * c) * (upper * lower)
            value = body + relaid[b, s] + DT_NL * (body * (body * plain - cross))
            relaid[b, s] = value
            total[b] = total[b] + value
        return tuple(total)

    empty = jnp.zeros((8, LANES), jnp.float32)
    total = lax.fori_loop(0, pairs, transfer, (empty,) * lots, unroll=TRANSFER)

    half = jnp.right_shift(lane, 6)
    sigma = [sigma_of(sub * (2 * lots) + 2 * b + half) for b in range(lots)]
    weight = 1.0 / (ndirs * NFREQ)

    def over_all(terms):
        x = jnp.sum(sum(terms), axis=0, keepdims=True)
        x = jnp.broadcast_to(x, (8, LANES))
        x = x + pltpu.roll(x, 64, 1)
        return x + pltpu.roll(x, 32, 1)

    etot = over_all(total) * weight
    inverse = over_all([x / y for x, y in zip(total, sigma)]) * weight
    msig = jnp.clip(etot / jnp.maximum(inverse, INV_FLOOR), SIG_LO, SIG_HI)
    steep = etot * (msig * msig * msig * msig) / APM
    rate = [CDS * ((x / msig) * (x / msig)) * msig * (steep * steep) for x in sigma]
    damp = [1.0 / (1.0 + x) for x in rate]
    speed = jnp.concatenate([wind_speed[...]] * 4, axis=1)
    wind = [speed * x for x in sigma]
    push = [BETA * x for x in sigma]
    towards = jnp.concatenate([wind_dir[...]] * 4, axis=1)
    step = lax.broadcasted_iota(jnp.int32, (pairs, LANES), 0) * 2 + jnp.bitwise_and(
        jnp.right_shift(lax.broadcasted_iota(jnp.int32, (pairs, LANES), 1), 5), 1
    )
    rows[...] = cosine((2.0 * math.pi / ndirs) * step.astype(jnp.float32) - towards)

    def grow(s, carry):
        along = rows[pl.ds(s, 1), :]
        for b in range(lots):
            growth = push[b] * jnp.maximum(wind[b] * along - 1.0, 0.0)
            value = relaid[b, s] * (1.0 + growth) * damp[b]
            quarter = pltpu.roll(value, LANES - 32, 1)
            even = jnp.where(low, value, quarter)
            odd = jnp.where(low, quarter, pltpu.roll(value, 64, 1))
            for i, part in enumerate((even, odd)):
                turned[pl.ds(b * ndirs + 2 * s + i, 8, stride=lots * ndirs), :] = part
        return carry

    low = lane < 32
    lax.fori_loop(0, pairs, grow, 0, unroll=GROW)

    def place(a, carry):
        for b in range(lots):
            spot = pl.ds(pl.multiple_of((a * lots + b) * ndirs, ndirs), ndirs)
            flat = jnp.swapaxes(turned[spot, :], 0, 1)
            for x in range(2):
                out[a * 2 * lots + 2 * b + x] = flat[32 * x : 32 * x + 32]
        spot = pl.ds(a * 2 * lots, 2 * lots)
        pltpu.make_async_copy(out.at[spot], out_at.at[spot], left.at[a]).start()
        return carry

    lax.fori_loop(0, 8, place, 0, unroll=PLACE)
    for a in range(8):
        spot = pl.ds(a * 2 * lots, 2 * lots)
        pltpu.make_async_copy(out.at[spot], out_at.at[spot], left.at[a]).wait()


def local_scoped(ndirs, *refs):
    freqs, dirs, npoints = refs[0].shape
    sums = [
        pltpu.ACC(unit)((3 * npoints // TILE, TILE), jnp.float32)
        for unit in range(2)
        for _ in range(2 * dirs * freqs // 3)
    ]
    pl.run_scoped(lambda *sums: local_kernel(ndirs, *refs, *sums), *sums)


def local_call(
    ndirs, parts, spectrum, neighbours, edge_angle, edge_coef, land_mask, space_order
):
    dirs, freqs, npoints = spectrum.shape
    tiles = npoints // TILE
    near = neighbours.shape[0]
    vmem = pl.BlockSpec(memory_space=pltpu.VMEM)
    return pl.pallas_call(
        functools.partial(local_scoped, ndirs),
        out_shape=jax.ShapeDtypeStruct((parts * dirs * freqs // 4, 2, LANES), jnp.bfloat16),
        in_specs=[pl.BlockSpec(memory_space=pltpu.MemorySpace.HBM)] * 6,
        out_specs=vmem,
        scratch_shapes=[
            pltpu.VMEM((freqs, dirs, npoints), jnp.float32),
            pltpu.VMEM((near, npoints), jnp.int32),
            pltpu.VMEM((near, npoints), jnp.float32),
            pltpu.VMEM((near, npoints), jnp.float32),
            pltpu.VMEM((1, npoints), jnp.int32),
            pltpu.VMEM((1, npoints), jnp.int32),
            pltpu.SemaphoreType.DMA((6,)),
            pltpu.VMEM((dirs, 8, npoints), jnp.float32),
            pltpu.VMEM((TILE // LANES, (dirs * freqs + 2) * tiles, LANES), jnp.float32),
            pltpu.VMEM((dirs * freqs * tiles, TILE), jnp.bfloat16),
            pltpu.VMEM((TILE // LANES, 2 * dirs * freqs * tiles + 8, LANES), jnp.float32),
            pltpu.VMEM((2 * dirs * freqs * tiles, TILE), jnp.bfloat16),
            pltpu.VMEM((TILE, TILE), jnp.bfloat16),
        ],
        compiler_params=pltpu.CompilerParams(vmem_limit_bytes=40 * 1024 * 1024),
        name="local_step",
    )(
        *(
            pltpu.with_memory_space_constraint(x, pltpu.MemorySpace.HBM)
            for x in (
                spectrum.transpose(1, 0, 2),
                neighbours,
                edge_angle,
                edge_coef,
                land_mask.reshape(1, npoints),
                space_order.reshape(1, npoints),
            )
        )
    )


def finish_call(ndirs, nd, nf, dia_offsets, dia_coef, wind_speed, wind_dir, blocks):
    vmem = pl.BlockSpec(memory_space=pltpu.VMEM)
    hbm = pl.BlockSpec(memory_space=pltpu.MemorySpace.HBM)
    lots = blocks.shape[0] // (nd * nf)
    return pl.pallas_call(
        functools.partial(finish_kernel, ndirs),
        out_shape=jax.ShapeDtypeStruct((NFREQ, LANES // 4, ndirs), jnp.float32),
        in_specs=[hbm, hbm, hbm, hbm, vmem],
        out_specs=pl.BlockSpec(memory_space=pltpu.MemorySpace.HBM),
        scratch_shapes=[
            pltpu.SMEM(dia_offsets.shape, jnp.int32),
            pltpu.SMEM(dia_coef.shape, jnp.float32),
            pltpu.VMEM(wind_speed.shape, jnp.float32),
            pltpu.VMEM(wind_dir.shape, jnp.float32),
            pltpu.SemaphoreType.DMA((4,)),
            pltpu.VMEM((2, 2, lots + 2, nd + DSPAN, nf, LANES), jnp.float32),
            pltpu.VMEM((lots, nd, nf, LANES), jnp.float32),
            pltpu.VMEM((nd, LANES), jnp.float32),
            pltpu.VMEM((2 * nf * lots * nd, LANES), jnp.float32),
            pltpu.VMEM((nf * lots * ndirs, LANES), jnp.float32),
            pltpu.VMEM((NFREQ, LANES // 4, ndirs), jnp.float32),
            pltpu.SemaphoreType.DMA((nf,)),
        ],
        compiler_params=pltpu.CompilerParams(vmem_limit_bytes=40 * 1024 * 1024),
        name="finish_step",
    )(
        *(
            pltpu.with_memory_space_constraint(x, pltpu.MemorySpace.HBM)
            for x in (dia_offsets, dia_coef, wind_speed, wind_dir)
        ),
        blocks,
    )


def on_device(
    spectrum,
    neighbours,
    edge_angle,
    edge_coef,
    land_mask,
    dia_offsets,
    dia_coef,
    space_order,
    wind_speed,
    wind_dir,
):
    dirs, freqs, npoints = spectrum.shape
    nd, nf = lax.axis_size("dir"), lax.axis_size("freq")
    parts = nd * nf
    blocks = local_call(
        nd * dirs, parts, spectrum, neighbours, edge_angle, edge_coef, land_mask, space_order
    )
    blocks = lax.all_to_all(blocks, ("dir", "freq"), split_axis=0, concat_axis=0, tiled=True)
    npts = npoints // parts
    done = finish_call(
        nd * dirs, nd, nf, dia_offsets, dia_coef,
        wind_speed.reshape(1, npts), wind_dir.reshape(1, npts), blocks,
    )
    return done.transpose(2, 0, 1)


def solution(mesh):
    in_specs = (
        P("dir", "freq", None),
        P(),
        P(),
        P(),
        P(),
        P(),
        P(),
        P(),
        P(("dir", "freq")),
        P(("dir", "freq")),
    )
    out_specs = P(None, None, ("dir", "freq"))
    return jax.shard_map(
        on_device, mesh=mesh, in_specs=in_specs, out_specs=out_specs, check_vma=False
    )
```
